32 devices in a mesh: row: 4 (over x, core), col: 8 (over z, y).
Axes of the slice: x: 2, y: 2, z: 4, core: 2. Of those that a mesh axis runs over, the one named last changes fastest.
Arguments:
- matrix: float32 [4096, 10240], P('row', 'col'), may hold values from -6 to 6
- panel_lower: float32 [8, 4096, 512], P('col', 'row'), may hold values from -0.25 to 0.25
- pivots: int32 [512], replicated, may hold values from 0 to 4095, as said below
- checks: float32 [10240], P('col'), may hold values from -6 to 6
Outputs:
- updated: float32 [4096, 10240], P('row', 'col')
- new_checks: float32 [10240], P('col')
The draws below stay inside these ranges and needn't reach their ends.
Inputs may be any that keep to these rules, and one draw needn't show every extreme that they name: `pivots`: the 512 entries are distinct; entry k is either k itself or a row of at least 512.
All inputs are finite; a program needn't handle non-finite values.
Results may differ from the reference program's by a relative error of at most 0.000073.
Values sent between devices are 32-bit elements; how exact they have to be, the bound alone decides.
No kernel may reach another device: no remote copies, remote signals or barrier semaphores. Data moves between devices by JAX's collectives and lax.ppermute only.
A program may use at most 128 MiB of HBM per device.

```python
import jax
import jax.numpy as jnp
from jax import lax

NB = 512
M = 4096
NC = 10240
N_COL = 8


def draw_pivots(key, part):
    order = jax.random.permutation(jax.random.fold_in(key, 11), M - NB) + NB
    keeper = jax.random.randint(jax.random.fold_in(key, 12), (NB,), 0, 4)
    return jnp.where(keeper == 0, jnp.arange(NB, dtype=jnp.int32), order[:NB].astype(jnp.int32)).astype(jnp.int32)


def levels(rng, extent, pieces, smallest, top_value):
    level, own = 1.0, jax.random.fold_in(rng, 6)
    for axis_at, parts in pieces:
        heights = jnp.exp(jax.random.uniform(jax.random.fold_in(own, axis_at), (parts,), jnp.float32, smallest / len(pieces), top_value / len(pieces)))
        level = level * jnp.repeat(heights, extent[axis_at] // parts).reshape([-1 if axis == axis_at else 1 for axis in range(len(extent))])
    return level


def normal_values(stream_key, shape, spread, limit, cuts=(), kind=jnp.bfloat16):
    loudness = levels(stream_key, shape, cuts, -0.22, 0.18) if cuts else 1.0
    entries = jax.random.normal(stream_key, shape, jnp.float32) * spread * loudness
    return jnp.minimum(jnp.maximum(entries, -limit), limit).astype(kind)


def setup_inputs(seed: int = 0) -> dict:
    key_list = jax.random.split(jax.random.key(seed), 5)
    matrix = normal_values(key_list[0], (M, NC), 1.0, 6.0, ((0, 4), (1, 8)), jnp.float32)
    panel_lower = normal_values(key_list[1], (N_COL, M, NB), NB ** -0.5, 0.25, ((0, 8), (1, 4)), jnp.float32)
    pivots = draw_pivots(jax.random.fold_in(key_list[4], 71), 0)
    checks = normal_values(key_list[3], (NC,), 1.0, 6.0, ((0, 8),), jnp.float32)
    return dict(matrix=matrix, panel_lower=panel_lower, pivots=pivots, checks=checks)


def reference(matrix, panel_lower, pivots, checks):
    owned = panel_lower[0]
    picked = matrix[pivots]
    swapped = matrix.at[pivots].set(matrix[:NB])
    unit = jnp.tril(owned[:NB], -1) + jnp.eye(NB, dtype=jnp.float32)
    solved = jax.scipy.linalg.solve_triangular(unit, picked, lower=True, unit_diagonal=True)
    lower = swapped[NB:] - jnp.dot(owned[NB:].astype(jnp.float32), solved.astype(jnp.float32), precision=lax.Precision.HIGHEST, preferred_element_type=jnp.float32)
    updated = jnp.concatenate([solved, lower], axis=0)
    change = lax.optimization_barrier(jnp.sum(picked, 0)) - lax.optimization_barrier(jnp.sum(solved, 0)) + lax.optimization_barrier(jnp.sum(swapped[NB:] - lower, 0))
    new_checks = checks - change / jnp.sqrt(jnp.float32(M))
    return (updated, new_checks)
```

```python
import functools

import jax
import jax.numpy as jnp
from jax import lax
from jax.experimental import pallas as pl
from jax.experimental.pallas import tpu as pltpu
from jax.sharding import PartitionSpec as P


BLOCK = 128
CHUNKS = 4
LAG = 1
HIGHEST = lax.Precision.HIGHEST


def split(x):
    hi = x.astype(jnp.bfloat16)
    return hi, (x - hi.astype(jnp.float32)).astype(jnp.bfloat16)


def bdot(a, b):
    return jnp.dot(a, b, preferred_element_type=jnp.float32)


def dot3(a, b):
    return bdot(a[0], b[1]) + bdot(a[1], b[0]) + bdot(a[0], b[0])


def fdot(a, b):
    return jnp.dot(a, b, precision=HIGHEST, preferred_element_type=jnp.float32)


def vmem():
    return pl.BlockSpec(memory_space=pltpu.VMEM)


def smem():
    return pl.BlockSpec(memory_space=pltpu.SMEM)


def gather_kernel(idx, m, o):
    def group(g, c):
        for i in range(8):
            k = g * 8 + i
            o[pl.ds(k, 1), :] = m[pl.ds(idx[k], 1), :]
        return c

    lax.fori_loop(0, o.shape[0] // 8, group, 0)


def scatter_kernel(dst, m, u, o):
    o[...] = m[...]

    def group(g, c):
        for i in range(8):
            k = g * 8 + i
            d = dst[k]

            @pl.when(d >= 0)
            def _():
                o[pl.ds(d, 1), :] = u[pl.ds(k, 1), :]

        return c

    lax.fori_loop(0, u.shape[0] // 8, group, 0)


def invert_kernel(u, o):
    n = BLOCK
    row = lax.broadcasted_iota(jnp.int32, (n, n), 0)
    col = lax.broadcasted_iota(jnp.int32, (n, n), 1)
    eye = jnp.where(row == col, 1.0, 0.0)
    count = u.shape[0] // n
    diag = [u[b * n : (b + 1) * n, b * n : (b + 1) * n] for b in range(count)]
    inv = None
    s = 1
    while s < n:
        mask = (row // (2 * s) == col // (2 * s)) & ((row // s) % 2 == 1) & ((col // s) % 2 == 0)
        low = [jnp.where(mask, d, 0.0) for d in diag]
        if inv is None:
            inv = [eye - c for c in low]
        else:
            right = [fdot(c, d) for c, d in zip(low, inv)]
            inv = [d - fdot(d, t) for d, t in zip(inv, right)]
        s *= 2
    for b in range(count):
        o[b * n : (b + 1) * n, :] = inv[b]


def place_kernel(rows, count, split_out, blk, *refs):
    bufs, outs = refs[:count], refs[count:]
    total = outs[0].shape[0] // rows

    def put(at, value):
        if split_out:
            hi, lo = split(value)
            outs[0][pl.ds(at, rows), :] = hi
            outs[1][pl.ds(at, rows), :] = lo
        else:
            outs[0][pl.ds(at, rows), :] = value

    for i in range(count - 1):

        @pl.when((blk[i] >= 0) & (blk[i] < total))
        def _(i=i):
            put(pl.multiple_of(blk[i] * rows, rows), bufs[i][...])

    @pl.when(blk[count - 1] >= 0)
    def _():
        for b in range(total):
            put(b * rows, bufs[count - 1][b * rows : (b + 1) * rows, :])


def final_kernel(scale, flag, p, u, inv, lhi, llo, w, sw, ck, o, nc, s_hi, s_lo, uh, ul, ih, il):
    nb = p.shape[0]
    n = BLOCK
    count = nb // n

    @pl.when(pl.program_id(0) == 0)
    def _():
        uh[...], ul[...] = split(u[...])
        ih[...], il[...] = split(inv[...])

    sums = jnp.zeros((1, p.shape[1]), jnp.float32)
    for b in range(count):
        rows = slice(b * n, (b + 1) * n)
        x = p[rows, :]
        sums += jnp.sum(x, 0, keepdims=True)
        for j in range(b):
            cols = slice(j * n, (j + 1) * n)
            x = x - dot3((uh[rows, cols], ul[rows, cols]), (s_hi[cols, :], s_lo[cols, :]))
        s = dot3((ih[rows, :], il[rows, :]), split(x))
        sums -= jnp.sum(s, 0, keepdims=True)
        s_hi[rows, :], s_lo[rows, :] = split(s)

        @pl.when(flag[0] == 1)
        def _(rows=rows, s=s):
            o[rows, :] = s

    solved = (s_hi[...], s_lo[...])
    sums += dot3(split(w[...]), solved)[0:1, :]
    nc[...] = ck[...] - sums * scale

    def update(at):
        rows = pl.ds(at, n)
        o[rows, :] = sw[rows, :] - dot3((lhi[rows, :], llo[rows, :]), solved)

    for b in range(sw.shape[0] // n):
        if b < count:

            @pl.when(flag[0] == 0)
            def _(b=b):
                update(b * n)

        else:
            update(b * n)


def stream(panel, n_col, chunks, lag):
    depth = n_col // 2
    col = lax.axis_index("col")
    is_root, is_side = col == 0, col == 1
    n = panel.shape[0] // (2 * chunks)
    a = [panel[2 * j * n : (2 * j + 1) * n] for j in range(chunks)]
    b = [panel[(2 * j + 1) * n : (2 * j + 2) * n] for j in range(chunks)]
    z, y = col // 2, col % 2
    along, across = {}, {}
    blocks = {}
    for t in range(max(chunks + lag * depth, 2 * chunks)):
        z_pairs, y_pairs = [], []
        for zz in range(depth):
            for yy in range(2):
                j = t - lag * zz - lag * yy
                if 0 <= j < chunks:
                    if zz < depth - 1:
                        z_pairs.append((2 * zz + yy, 2 * zz + 2 + yy))
                    if zz > 0:
                        y_pairs.append((2 * zz + yy, 2 * zz + 1 - yy))
        if t < 2 * chunks:
            y_pairs.append((0, 1))
        before_z, before_y = along.get(t - lag), across.get(t - lag)
        if t < chunks:
            z_in = b[t] if before_z is None else jnp.where(is_root, b[t], before_z)
        else:
            z_in = before_z
        if z_in is not None and before_y is not None:
            z_in = jnp.where(is_side, before_y, z_in)
        head = a[t] if t < chunks else (b[t - chunks] if t < 2 * chunks else None)
        if head is None:
            y_in = z_in
        elif z_in is None:
            y_in = head
        else:
            y_in = jnp.where(is_root, head, z_in)
        if y_pairs:
            across[t] = lax.ppermute(y_in, "col", y_pairs)
            j = t - lag * z - lag * (1 - y)
            ok = (z > 0) & (j >= 0) & (j < chunks)
            value = jnp.where(ok, 2 * j + y, -1)
            if t < 2 * chunks:
                first = 2 * t if t < chunks else 2 * (t - chunks) + 1
                value = jnp.where(is_side, first, value)
            blocks["y", t] = value
        if z_pairs:
            along[t] = lax.ppermute(z_in, "col", z_pairs)
            j = t - lag * (z - 1) - lag * y
            ok = (z > 0) & (j >= 0) & (j < chunks)
            blocks["z", t] = jnp.where(ok, 2 * j + 1 - y, -1)
    return n, along, across, blocks, is_root


def place(panel, rows, total_rows, entries, is_root, split_out):
    bufs = [e[0] for e in entries] + [panel]
    blk = jnp.stack([e[1] for e in entries] + [jnp.where(is_root, 0, -1)]).astype(jnp.int32)
    shape = (total_rows, panel.shape[1])
    if split_out:
        out = (jax.ShapeDtypeStruct(shape, jnp.bfloat16),) * 2
        specs = (vmem(), vmem())
    else:
        out, specs = (jax.ShapeDtypeStruct(shape, jnp.float32),), (vmem(),)
    return pl.pallas_call(
        functools.partial(place_kernel, rows, len(bufs), split_out),
        out_shape=out,
        in_specs=[smem()] + [vmem()] * len(bufs),
        out_specs=specs,
        cost_estimate=pl.CostEstimate(flops=0, bytes_accessed=8 * total_rows * panel.shape[1], transcendentals=0),
    )(blk, *bufs)


def halves(own, other, high):
    return jnp.concatenate(
        [jnp.where(high, other, own), jnp.where(high, own, other)], axis=0
    )


def local(matrix, panel_lower, pivots, checks):
    local_rows, local_cols = matrix.shape
    nb = pivots.shape[0]
    n_row, n_col = lax.axis_size("row"), lax.axis_size("col")
    row, col = lax.axis_index("row"), lax.axis_index("col")
    panel = panel_lower[0]
    high = (row % 2) == 1
    owner = pivots // local_rows
    local_index = pivots - row * local_rows
    mine = owner == row

    rows, along, across, blocks, is_root = stream(panel, n_col, CHUNKS, LAG)

    global_rows = row * local_rows + jnp.arange(local_rows, dtype=jnp.int32)
    weights = jnp.sum(jnp.where((global_rows >= nb)[:, None], panel, 0.0), 0, keepdims=True)
    weights = jnp.broadcast_to(weights, (8, nb))
    bit = 1
    while bit < n_row:
        weights += lax.ppermute(weights, "row", [(i, i ^ bit) for i in range(n_row)])
        bit *= 2
    bit = 1
    while bit < n_col:
        moved = lax.ppermute(weights, "col", [(i, i + bit) for i in range(bit)])
        weights = jnp.where((col >= bit) & (col < 2 * bit), moved, weights)
        bit *= 2

    index = jnp.where(mine, local_index, jnp.arange(nb, dtype=jnp.int32))
    picked = pl.pallas_call(
        gather_kernel,
        out_shape=jax.ShapeDtypeStruct((nb, local_cols), jnp.float32),
        in_specs=[smem(), vmem()],
        out_specs=vmem(),
        cost_estimate=pl.CostEstimate(flops=0, bytes_accessed=8 * matrix.size, transcendentals=0),
    )(index, matrix)
    upper = matrix[:nb]
    half = nb // 2
    swap_all = [(i, i ^ 1) for i in range(n_row)]
    bit, level = 1, 0
    while bit < n_row:
        pairs = [(i, i ^ bit) for i in range(n_row)]
        if bit == 1:
            other = lax.ppermute(picked, "row", pairs)
        else:
            piece = lax.dynamic_slice_in_dim(picked, jnp.where(high, half, 0), half, 0)
            piece = lax.ppermute(piece, "row", pairs)
            other = halves(piece, lax.ppermute(piece, "row", swap_all), high)
        group = row >> level
        upper = jnp.where(group == 1, other, upper)
        theirs = (owner >> level) == (group ^ 1)
        outside = (owner >> level) != group
        take = theirs | (outside & (group == 1))
        picked = jnp.where(take[:, None], other, picked)
        bit, level = 2 * bit, level + 1

    target = jnp.where(mine & (pivots >= nb), local_index, -1)
    swapped = pl.pallas_call(
        scatter_kernel,
        out_shape=jax.ShapeDtypeStruct(matrix.shape, jnp.float32),
        in_specs=[smem(), vmem(), vmem()],
        out_specs=vmem(),
        cost_estimate=pl.CostEstimate(flops=0, bytes_accessed=8 * matrix.size, transcendentals=0),
    )(target, matrix, upper)

    last = CHUNKS + LAG * (n_col // 2)
    keep = nb // rows // 2
    early = []
    for (kind, t), value in blocks.items():
        limit = keep + LAG * (n_col // 2)
        if kind == "y" and (t < limit or CHUNKS <= t < CHUNKS + keep):
            early.append((across[t], value))
        if kind == "z" and t < limit - LAG:
            early.append((along[t], value))
    (diag,) = place(panel, rows, nb, early, is_root, False)
    moved = lax.ppermute(diag, "row", [(0, 1)])
    diag = jnp.where(row == 1, moved, diag)
    bit = 2
    while bit < n_row:
        piece = lax.dynamic_slice_in_dim(diag, jnp.where(high, half, 0), half, 0)
        piece = lax.ppermute(piece, "row", [(i, i + bit) for i in range(bit)])
        other = lax.ppermute(piece, "row", [(i, i ^ 1) for i in range(bit, 2 * bit)])
        diag = jnp.where((row >= bit) & (row < 2 * bit), halves(piece, other, high), diag)
        bit *= 2
    inverse = pl.pallas_call(
        invert_kernel,
        out_shape=jax.ShapeDtypeStruct((nb, BLOCK), jnp.float32),
        in_specs=[vmem()],
        out_specs=vmem(),
        cost_estimate=pl.CostEstimate(flops=10**9, bytes_accessed=nb * nb * 4, transcendentals=0),
    )(diag)

    entries = [((across if kind == "y" else along)[t], value) for (kind, t), value in blocks.items()]
    lower_hi, lower_lo = place(panel, rows, local_rows, entries, is_root, True)

    width = 256 if local_cols % 256 == 0 else local_cols
    scale = 1.0 / float((local_rows * n_row) ** 0.5)
    whole = lambda shape: pl.BlockSpec(shape, lambda i: (0, 0))
    strip = lambda height: pl.BlockSpec((height, width), lambda i: (0, i))
    bf = jnp.bfloat16
    updated, new_checks = pl.pallas_call(
        functools.partial(final_kernel, scale),
        grid=(local_cols // width,),
        out_shape=(
            jax.ShapeDtypeStruct(matrix.shape, jnp.float32),
            jax.ShapeDtypeStruct((1, local_cols), jnp.float32),
        ),
        in_specs=[
            smem(),
            strip(nb),
            whole((nb, nb)),
            whole((nb, BLOCK)),
            whole((local_rows, nb)),
            whole((local_rows, nb)),
            whole((8, nb)),
            strip(local_rows),
            strip(1),
        ],
        out_specs=(strip(local_rows), strip(1)),
        scratch_shapes=[
            pltpu.VMEM((nb, width), bf),
            pltpu.VMEM((nb, width), bf),
            pltpu.VMEM((nb, nb), bf),
            pltpu.VMEM((nb, nb), bf),
            pltpu.VMEM((nb, BLOCK), bf),
            pltpu.VMEM((nb, BLOCK), bf),
        ],
    )(
        jnp.where(row == 0, 1, 0).astype(jnp.int32)[None],
        picked,
        diag,
        inverse,
        lower_hi,
        lower_lo,
        weights,
        swapped,
        checks[None, :],
    )
    return updated, new_checks[0]


def solution(mesh):
    return jax.shard_map(
        local,
        mesh=mesh,
        in_specs=(P("row", "col"), P("col", "row", None), P(), P("col")),
        out_specs=(P("row", "col"), P("col")),
        check_vma=False,
    )
```

```python
import functools

import jax
import jax.numpy as jnp
from jax import lax
from jax.experimental import pallas as pl
from jax.experimental.pallas import tpu as pltpu
from jax.sharding import PartitionSpec as P


BLOCK = 128
CHUNKS = 4
LAG = 1
HIGHEST = lax.Precision.HIGHEST


def split(x):
    hi = x.astype(jnp.bfloat16)
    return hi, (x - hi.astype(jnp.float32)).astype(jnp.bfloat16)


def bdot(a, b):
    return jnp.dot(a, b, preferred_element_type=jnp.float32)


def fdot(a, b):
    return jnp.dot(a, b, precision=HIGHEST, preferred_element_type=jnp.float32)


def vmem():
    return pl.BlockSpec(memory_space=pltpu.VMEM)


def smem():
    return pl.BlockSpec(memory_space=pltpu.SMEM)


def gather_kernel(idx, m, o):
    def group(g, c):
        for i in range(8):
            k = g * 8 + i
            o[pl.ds(k, 1), :] = m[pl.ds(idx[k], 1), :]
        return c

    lax.fori_loop(0, o.shape[0] // 8, group, 0)


def move_rows(dst, listed, u, o):
    def note(k, found):
        listed[found] = k
        return found + (dst[k] >= 0).astype(jnp.int32)

    found = lax.fori_loop(0, u.shape[0], note, 0, unroll=8)

    def one(i, c):
        k = listed[i]
        o[pl.ds(dst[k], 1), :] = u[pl.ds(k, 1), :]
        return c

    lax.fori_loop(0, found, one, 0)


def scatter_kernel(dst, m, u, o, listed):
    o[...] = m[...]
    move_rows(dst, listed, u, o)


def merge_kernel(rank, dst, mask, m, x, base, p0, p1, q0, q1, o, picked, full, up, listed, sems):
    half, quarter = full.shape[0] // 2, p0.shape[0]
    nb = full.shape[0]
    mine = (rank[0] % 2) * half
    copies = [pltpu.make_async_copy(m, o, sems.at[0]), pltpu.make_async_copy(x, picked, sems.at[1])]
    for i, (near, far) in enumerate(((p0, q0), (p1, q1))):
        for k, (piece, first) in enumerate(((near, mine), (far, half - mine))):
            place = pl.ds(pl.multiple_of(first + i * quarter, quarter), quarter)
            copies.append(pltpu.make_async_copy(piece, full.at[place, :], sems.at[2 + 2 * i + k]))
    for copy in copies:
        copy.start()

    @pl.when(rank[0] == 0)
    def _():
        copy = pltpu.make_async_copy(m.at[pl.ds(0, nb), :], up, sems.at[6])
        copy.start()
        copy.wait()

    @pl.when(rank[0] == 1)
    def _():
        copy = pltpu.make_async_copy(base, up, sems.at[6])
        copy.start()
        copy.wait()

    for copy in copies:
        copy.wait()
    theirs = mask[...] != 0
    picked[...] = jnp.where(theirs, full[...], picked[...])

    @pl.when(rank[0] < 2)
    def _():
        move_rows(dst, listed, up, o)

    @pl.when(rank[0] >= 2)
    def _():
        move_rows(dst, listed, full, o)


def invert_kernel(u, o):
    n = BLOCK
    row = lax.broadcasted_iota(jnp.int32, (n, n), 0)
    col = lax.broadcasted_iota(jnp.int32, (n, n), 1)
    eye = jnp.where(row == col, 1.0, 0.0)
    count = u.shape[0] // n
    diag = [u[b * n : (b + 1) * n, b * n : (b + 1) * n] for b in range(count)]
    inv = None
    s = 1
    while s < n:
        mask = (row // (2 * s) == col // (2 * s)) & ((row // s) % 2 == 1) & ((col // s) % 2 == 0)
        low = [jnp.where(mask, d, 0.0) for d in diag]
        if inv is None:
            inv = [eye - c for c in low]
        else:
            right = [fdot(c, d) for c, d in zip(low, inv)]
            inv = [d - fdot(d, t) for d, t in zip(inv, right)]
        s *= 2
    for b in range(count):
        o[b * n : (b + 1) * n, :] = inv[b]


def fetch_kernel(want, blk, *refs):
    *bufs, panel, o, sem = refs
    for i, buf in enumerate(bufs):

        @pl.when(blk[i] == want)
        def _(buf=buf):
            copy = pltpu.make_async_copy(buf, o, sem)
            copy.start()
            copy.wait()

    @pl.when(blk[len(bufs)] == 0)
    def _():
        rows = o.shape[0]
        copy = pltpu.make_async_copy(panel.at[pl.ds(want * rows, rows), :], o, sem)
        copy.start()
        copy.wait()


def split_kernel(rows, blk, *refs):
    *bufs, panel, o, stage, sems = refs
    total = panel.shape[0]

    def copies(do):
        for i, buf in enumerate(bufs):

            @pl.when(blk[i] >= 0)
            def _(i=i, buf=buf):
                place = pl.ds(pl.multiple_of(blk[i] * rows, rows), rows)
                do(pltpu.make_async_copy(buf, stage.at[place, :], sems.at[i]))

        @pl.when(blk[len(bufs)] == 0)
        def _():
            do(pltpu.make_async_copy(panel, stage, sems.at[len(bufs)]))

    copies(lambda copy: copy.start())
    copies(lambda copy: copy.wait())
    n = BLOCK
    for r in range(0, total, n):
        for k in range(panel.shape[1] // n):
            o[r : r + n, 3 * n * k : 3 * n * (k + 1)] = wide(stage[r : r + n, k * n : (k + 1) * n])


def wide(x):
    hi, lo = split(x)
    return jnp.concatenate([hi, hi, lo], axis=1)


def tall(x):
    hi, lo = split(x)
    return jnp.concatenate([hi, lo, hi], axis=0)


def final_kernel(scale, strip, flag, p, u, inv, ll_in, w, sw_in, ck, o, nc, s3, uu, ii, ob, ll, sw, got, sent):
    arrivals = [pltpu.make_async_copy(ll_in, ll, got.at[0]), pltpu.make_async_copy(sw_in, sw, got.at[1])]
    for copy in arrivals:
        copy.start()
    nb, cols = p.shape
    n = BLOCK
    count = nb // n
    for b in range(count):
        rows = slice(b * n, (b + 1) * n)
        ii[rows, :] = wide(inv[rows, :])
        for k in range(b):
            uu[rows, 3 * n * k : 3 * n * (k + 1)] = wide(u[rows, k * n : (k + 1) * n])
    for b in range(count):
        rows = slice(b * n, (b + 1) * n)
        for c in range(0, cols, strip):
            at = slice(c, c + strip)
            x = p[rows, at]
            if b:
                x = x - bdot(uu[rows, : 3 * n * b], s3[: 3 * n * b, at])
            solved = bdot(ii[rows, :], tall(x))
            s3[3 * n * b : 3 * n * (b + 1), at] = tall(solved)
            ob[rows, at] = solved
    for copy in arrivals:
        copy.wait()
    wrows = jnp.concatenate([wide(w[:, k * n : (k + 1) * n]) for k in range(count)], axis=1)
    is_top = flag[0] == 1
    leaving = []
    for c in range(0, cols, strip):
        at = slice(c, c + strip)
        sums = jnp.sum(p[:, at] - ob[:nb, at], 0, keepdims=True) + bdot(wrows, s3[:, at])[0:1, :]
        nc[:, at] = ck[:, at] - sums * scale
        for r in range(0, sw.shape[0], nb):
            rows = slice(r, r + nb)
            value = sw[rows, at] - bdot(ll[rows, :], s3[:, at])
            if r == 0:
                value = jnp.where(is_top, ob[rows, at], value)
            ob[rows, at] = value
            copy = pltpu.make_async_copy(ob.at[rows, at], o.at[rows, at], sent.at[len(leaving)])
            copy.start()
            leaving.append(copy)
    for copy in leaving:
        copy.wait()


def stream(panel, n_col, chunks, lag):
    depth = n_col // 2
    col = lax.axis_index("col")
    is_root, is_side = col == 0, col == 1
    n = panel.shape[0] // (2 * chunks)
    a = [panel[2 * j * n : (2 * j + 1) * n] for j in range(chunks)]
    b = [panel[(2 * j + 1) * n : (2 * j + 2) * n] for j in range(chunks)]
    z, y = col // 2, col % 2
    along, across = {}, {}
    blocks = {}
    for t in range(max(chunks + lag * depth, 2 * chunks)):
        z_pairs, y_pairs = [], []
        for zz in range(depth):
            for yy in range(2):
                j = t - lag * zz - lag * yy
                if 0 <= j < chunks:
                    if zz < depth - 1:
                        z_pairs.append((2 * zz + yy, 2 * zz + 2 + yy))
                    if zz > 0:
                        y_pairs.append((2 * zz + yy, 2 * zz + 1 - yy))
        if t < 2 * chunks:
            y_pairs.append((0, 1))
        before_z, before_y = along.get(t - lag), across.get(t - lag)
        if t < chunks:
            z_in = b[t] if before_z is None else jnp.where(is_root, b[t], before_z)
        else:
            z_in = before_z
        if z_in is not None and before_y is not None:
            z_in = jnp.where(is_side, before_y, z_in)
        head = a[t] if t < chunks else (b[t - chunks] if t < 2 * chunks else None)
        if head is None:
            y_in = z_in
        elif z_in is None:
            y_in = head
        else:
            y_in = jnp.where(is_root, head, z_in)
        if y_pairs:
            across[t] = lax.ppermute(y_in, "col", y_pairs)
            j = t - lag * z - lag * (1 - y)
            ok = (z > 0) & (j >= 0) & (j < chunks)
            value = jnp.where(ok, 2 * j + y, -1)
            if t < 2 * chunks:
                first = 2 * t if t < chunks else 2 * (t - chunks) + 1
                value = jnp.where(is_side, first, value)
            blocks["y", t] = value
        if z_pairs:
            along[t] = lax.ppermute(z_in, "col", z_pairs)
            j = t - lag * (z - 1) - lag * y
            ok = (z > 0) & (j >= 0) & (j < chunks)
            blocks["z", t] = jnp.where(ok, 2 * j + 1 - y, -1)
    return n, along, across, blocks, is_root


def anyspace():
    return pl.BlockSpec(memory_space=pl.ANY)


def fetch(blk, bufs, want):
    rows = bufs[0].shape[0]
    return pl.pallas_call(
        functools.partial(fetch_kernel, want),
        out_shape=jax.ShapeDtypeStruct((rows, bufs[0].shape[1]), jnp.float32),
        in_specs=[smem()] + [anyspace()] * len(bufs),
        out_specs=vmem(),
        scratch_shapes=[pltpu.SemaphoreType.DMA],
        cost_estimate=pl.CostEstimate(flops=0, bytes_accessed=8 * bufs[0].size, transcendentals=0),
    )(blk, *bufs)


def split_panel(blk, bufs):
    rows, panel = bufs[0].shape[0], bufs[-1]
    return pl.pallas_call(
        functools.partial(split_kernel, rows),
        out_shape=jax.ShapeDtypeStruct((panel.shape[0], 3 * panel.shape[1]), jnp.bfloat16),
        in_specs=[smem()] + [anyspace()] * len(bufs),
        out_specs=vmem(),
        scratch_shapes=[pltpu.VMEM(panel.shape, jnp.float32), pltpu.SemaphoreType.DMA((len(bufs),))],
        cost_estimate=pl.CostEstimate(flops=0, bytes_accessed=10 * panel.size, transcendentals=0),
    )(blk, *bufs)


def halves(own, other, high):
    return jnp.concatenate(
        [jnp.where(high, other, own), jnp.where(high, own, other)], axis=0
    )


def scatter_rows(target, matrix, upper):
    return pl.pallas_call(
        scatter_kernel,
        out_shape=jax.ShapeDtypeStruct(matrix.shape, jnp.float32),
        in_specs=[smem(), vmem(), vmem()],
        out_specs=vmem(),
        scratch_shapes=[pltpu.SMEM((upper.shape[0] + 8,), jnp.int32)],
        cost_estimate=pl.CostEstimate(flops=0, bytes_accessed=8 * matrix.size, transcendentals=0),
    )(target, matrix, upper)


def targets(pivots, row, local_rows):
    mine = (pivots // local_rows == row) & (pivots >= pivots.shape[0])
    return jnp.where(mine, pivots - row * local_rows, -1)


def gather_rows(index, matrix):
    return pl.pallas_call(
        gather_kernel,
        out_shape=jax.ShapeDtypeStruct((index.shape[0], matrix.shape[1]), jnp.float32),
        in_specs=[smem(), vmem()],
        out_specs=vmem(),
        cost_estimate=pl.CostEstimate(flops=0, bytes_accessed=8 * matrix.size, transcendentals=0),
    )(index, matrix)


def panel_sums(panel, row, nb):
    local_rows = panel.shape[0]
    global_rows = row * local_rows + jnp.arange(local_rows, dtype=jnp.int32)
    sums = jnp.sum(jnp.where((global_rows >= nb)[:, None], panel, 0.0), 0, keepdims=True)
    return jnp.broadcast_to(sums, (8, nb))


def exchange(panel, matrix, pivots):
    nb = pivots.shape[0]
    local_rows = matrix.shape[0]
    n_row, n_col = lax.axis_size("row"), lax.axis_size("col")
    row, col = lax.axis_index("row"), lax.axis_index("col")
    high = (row % 2) == 1
    owner = pivots // local_rows
    mine = owner == row
    rows, along, across, blocks, is_root = stream(panel, n_col, CHUNKS, LAG)
    weights = panel_sums(panel, row, nb)
    bit = 1
    while bit < n_row:
        weights += lax.ppermute(weights, "row", [(i, i ^ bit) for i in range(n_row)])
        bit *= 2
    bit = 1
    while bit < n_col:
        moved = lax.ppermute(weights, "col", [(i, i + bit) for i in range(bit)])
        weights = jnp.where((col >= bit) & (col < 2 * bit), moved, weights)
        bit *= 2
    index = jnp.where(mine, pivots - row * local_rows, jnp.arange(nb, dtype=jnp.int32))
    picked = gather_rows(index, matrix)
    upper = matrix[:nb]
    half = nb // 2
    swap_all = [(i, i ^ 1) for i in range(n_row)]
    bit, level = 1, 0
    while bit < n_row:
        pairs = [(i, i ^ bit) for i in range(n_row)]
        if bit == 1:
            other = lax.ppermute(picked, "row", pairs)
        else:
            piece = lax.dynamic_slice_in_dim(picked, jnp.where(high, half, 0), half, 0)
            piece = lax.ppermute(piece, "row", pairs)
            other = halves(piece, lax.ppermute(piece, "row", swap_all), high)
        group = row >> level
        upper = jnp.where(group == 1, other, upper)
        theirs = (owner >> level) == (group ^ 1)
        outside = (owner >> level) != group
        picked = jnp.where((theirs | (outside & (group == 1)))[:, None], other, picked)
        bit, level = 2 * bit, level + 1
    blk = jnp.stack(list(blocks.values()) + [jnp.where(is_root, 0, -1)]).astype(jnp.int32)
    bufs = [(across if kind == "y" else along)[t] for kind, t in blocks] + [panel]
    diag = jnp.concatenate([fetch(blk, bufs, b) for b in range(nb // rows)], 0)
    moved = lax.ppermute(diag, "row", [(0, 1)])
    diag = jnp.where(row == 1, moved, diag)
    bit = 2
    while bit < n_row:
        piece = lax.dynamic_slice_in_dim(diag, jnp.where(high, half, 0), half, 0)
        piece = lax.ppermute(piece, "row", [(i, i + bit) for i in range(bit)])
        other = lax.ppermute(piece, "row", [(i, i ^ 1) for i in range(bit, 2 * bit)])
        diag = jnp.where((row >= bit) & (row < 2 * bit), halves(piece, other, high), diag)
        bit *= 2
    swapped = scatter_rows(targets(pivots, row, local_rows), matrix, upper)
    return (blk, bufs), weights, picked, swapped, diag


def fence(*values):
    return lax.optimization_barrier(values)


def merge(row, target, theirs, matrix, picked, base, own, other):
    nb = picked.shape[0]
    return pl.pallas_call(
        merge_kernel,
        out_shape=(
            jax.ShapeDtypeStruct(matrix.shape, jnp.float32),
            jax.ShapeDtypeStruct(picked.shape, jnp.float32),
        ),
        in_specs=[smem(), smem(), vmem()] + [anyspace()] * 7,
        out_specs=(vmem(), vmem()),
        scratch_shapes=[
            pltpu.VMEM(picked.shape, jnp.float32),
            pltpu.VMEM(picked.shape, jnp.float32),
            pltpu.SMEM((nb + 8,), jnp.int32),
            pltpu.SemaphoreType.DMA((7,)),
        ],
        cost_estimate=pl.CostEstimate(flops=0, bytes_accessed=16 * matrix.size, transcendentals=0),
    )(row[None].astype(jnp.int32), target, theirs.astype(jnp.int32)[:, None], matrix, picked, base, *own, *other)


def exchange_4x8(panel, matrix, pivots):
    nb = pivots.shape[0]
    local_rows = matrix.shape[0]
    row, col = lax.axis_index("row"), lax.axis_index("col")
    z = col // 2
    high = (row % 2) == 1
    is_root, is_side = col == 0, col == 1
    n = local_rows // 4
    q = [panel[i * n : (i + 1) * n] for i in range(4)]
    at = lambda zz, yy: 2 * zz + yy
    owner = pivots // local_rows
    mine = owner == row
    index = jnp.where(mine, pivots - row * local_rows, jnp.arange(nb, dtype=jnp.int32))
    half = nb // 2
    quarter = half // 2
    core = [(i, i ^ 1) for i in range(4)]
    across_x = [(i, i ^ 2) for i in range(4)]
    send = lambda x, pairs: lax.ppermute(x, "row", pairs)
    r, s = at(0, 0), at(0, 1)
    plan_dn = [
        [(r, at(2, 0), 1)],
        [(r, at(2, 0), 3), (s, at(2, 1), 0), (at(2, 0), at(1, 0), 1)],
        [(r, at(2, 0), 2), (s, at(2, 1), 2), (at(2, 0), at(1, 0), 3), (at(2, 1), at(1, 1), 0)],
        [(at(2, 0), at(1, 0), 2), (at(2, 1), at(1, 1), 2)],
    ]
    plan_n3 = [
        [],
        [(at(2, 0), at(3, 0), 1)],
        [(at(2, 0), at(3, 0), 3), (at(2, 1), at(3, 1), 0)],
        [(at(2, 0), at(3, 0), 2), (at(2, 1), at(3, 1), 2)],
    ]
    plan_y = [
        [(r, s, 0)],
        [(r, s, 2), (at(2, 0), at(2, 1), 1)],
        [(r, s, 1), (at(2, 0), at(2, 1), 3), (at(2, 1), at(2, 0), 0)]
        + [(at(zz, 0), at(zz, 1), 1) for zz in (1, 3)],
        [(r, s, 3)]
        + [(at(zz, 0), at(zz, 1), 3) for zz in (1, 3)]
        + [(at(zz, 1), at(zz, 0), 0) for zz in (1, 3)],
    ]
    root_v, root_w = [1, 3, 2, None], [0, 2, 1, 3]
    dn, n3, ys = {}, {}, {}
    order, table = [], []

    def move(value, plan, kind, t):
        order.append((kind, t))
        line = [-1] * 8
        for _, target, block in plan:
            line[target] = block
        table.append(line)
        return lax.ppermute(value, "col", [(a, b) for a, b, _ in plan])

    def have(last):
        made = {"dn": dn, "n3": n3, "y": ys}
        keys = [i for i, (_, t) in enumerate(order) if t <= last]
        lines = jnp.asarray([table[i] for i in keys] + [[0] + [-1] * 7], jnp.int32)
        block = lax.dynamic_index_in_dim(lines, col, 1, False)
        return block, [made[order[i][0]][order[i][1]] for i in keys] + [panel]

    weights = panel_sums(panel, row, nb)
    own, other = [], []
    for t in range(4):
        if t == 0:
            v, w = q[1], q[0]
        else:
            v = dn[t - 1] if t == 3 else jnp.where(is_side, ys[t - 1], dn[t - 1])
            w = jnp.where(z == 3, n3[t - 1], dn[t - 1]) if t > 1 else dn[0]
            w = jnp.where(is_root, q[root_w[t]], w)
            if root_v[t] is not None:
                v = jnp.where(is_root, q[root_v[t]], v)
        dn[t] = move(v, plan_dn[t], "dn", t)
        if plan_n3[t]:
            n3[t] = move(v, plan_n3[t], "n3", t)
        ys[t] = move(w, plan_y[t], "y", t)
        if t == 0:
            for bit in (1, 2):
                weights += send(weights, [(i, i ^ bit) for i in range(4)])
        else:
            bit = 1 << (t - 1)
            moved = lax.ppermute(weights, "col", [(i, i + bit) for i in range(bit)])
            weights = jnp.where((col >= bit) & (col < 2 * bit), moved, weights)
        extra = [weights]
        if t == 0:
            picked = gather_rows(index, matrix)
            base = send(picked, core)
            extra += [picked, base]
        if t in (1, 2):
            if t == 1:
                theirs = owner == (row ^ 1)
                outside = (owner != row) & (row == 1)
                picked = jnp.where((theirs | outside)[:, None], base, picked)
            start = jnp.where(high, half, 0) + (t - 1) * quarter
            piece = lax.dynamic_slice_in_dim(picked, start, quarter, 0)
            own.append(send(piece, across_x))
            extra.append(own[-1])
        if t in (2, 3):
            other.append(send(own[t - 2], core))
            extra.append(other[-1])
        if t == 3:
            diag1 = fetch(*have(2), 1)
            far1 = send(diag1, [(0, 2)])
            theirs = (owner >> 1) != (row >> 1)
            swapped, picked = merge(
                row, targets(pivots, row, local_rows), theirs, matrix, picked, base, own, other
            )
            extra += [diag1, far1, swapped, picked]
        groups = [d for d in (dn, n3, ys) if t in d]
        fenced = list(fence(*[d[t] for d in groups], *extra))
        for d in groups:
            d[t] = fenced.pop(0)
        weights = fenced.pop(0)
        if t == 0:
            picked, base = fenced
        elif t == 1:
            own[0] = fenced[0]
        elif t == 2:
            own[1], other[0] = fenced
        else:
            other[1], diag1, far1, swapped, picked = fenced
    everything = have(3)
    diag0 = fetch(*everything, 0)[:, :half]
    far0 = send(diag0, [(0, 2)])
    near1 = send(jnp.where(row == 2, far1, diag1), [(0, 1), (2, 3)])
    diag0 = jnp.where(row == 2, far0, diag0)
    near0 = send(diag0, [(0, 1), (2, 3)])
    diag0 = jnp.where(high, near0, diag0)
    diag1 = jnp.where(high, near1, jnp.where(row == 2, far1, diag1))
    diag = jnp.concatenate([jnp.pad(diag0, ((0, 0), (0, nb - half))), diag1], 0)
    return everything, weights, picked, swapped, diag


def local(matrix, panel_lower, pivots, checks):
    local_rows, local_cols = matrix.shape
    nb = pivots.shape[0]
    n_row, n_col = lax.axis_size("row"), lax.axis_size("col")
    row = lax.axis_index("row")
    special = n_row == 4 and n_col == 8 and nb == local_rows // 2
    run = exchange_4x8 if special else exchange
    pieces, weights, picked, swapped, diag = run(panel_lower[0], matrix, pivots)
    inverse = pl.pallas_call(
        invert_kernel,
        out_shape=jax.ShapeDtypeStruct((nb, BLOCK), jnp.float32),
        in_specs=[vmem()],
        out_specs=vmem(),
        cost_estimate=pl.CostEstimate(flops=10**9, bytes_accessed=nb * nb * 4, transcendentals=0),
    )(diag)
    lower = split_panel(*pieces)
    strip = 256 if local_cols % 256 == 0 else local_cols
    scale = 1.0 / float((local_rows * n_row) ** 0.5)
    bf = jnp.bfloat16
    updated, new_checks = pl.pallas_call(
        functools.partial(final_kernel, scale, strip),
        out_shape=(
            jax.ShapeDtypeStruct(matrix.shape, jnp.float32),
            jax.ShapeDtypeStruct((1, local_cols), jnp.float32),
        ),
        in_specs=[smem()] + [vmem()] * 3 + [anyspace(), vmem(), anyspace(), vmem()],
        out_specs=(anyspace(), vmem()),
        scratch_shapes=[
            pltpu.VMEM((3 * nb, local_cols), bf),
            pltpu.VMEM((nb, 3 * nb), bf),
            pltpu.VMEM((nb, 3 * BLOCK), bf),
            pltpu.VMEM(matrix.shape, jnp.float32),
            pltpu.VMEM(lower.shape, bf),
            pltpu.VMEM(matrix.shape, jnp.float32),
            pltpu.SemaphoreType.DMA((2,)),
            pltpu.SemaphoreType.DMA((local_cols // strip * (local_rows // nb),)),
        ],
    )(
        jnp.where(row == 0, 1, 0).astype(jnp.int32)[None],
        picked,
        diag,
        inverse,
        lower,
        weights,
        swapped,
        checks[None, :],
    )
    return updated, new_checks[0]


def solution(mesh):
    return jax.shard_map(
        local,
        mesh=mesh,
        in_specs=(P("row", "col"), P("col", "row", None), P(), P("col")),
        out_specs=(P("row", "col"), P("col")),
        check_vma=False,
    )
```

```python
import functools

import jax
import jax.numpy as jnp
from jax import lax
from jax.experimental import pallas as pl
from jax.experimental.pallas import tpu as pltpu
from jax.sharding import PartitionSpec as P


BLOCK = 128
CHUNKS = 4
LAG = 1
HIGHEST = lax.Precision.HIGHEST


def split(x):
    hi = x.astype(jnp.bfloat16)
    return hi, (x - hi.astype(jnp.float32)).astype(jnp.bfloat16)


def bdot(a, b):
    return jnp.dot(a, b, preferred_element_type=jnp.float32)


def fdot(a, b):
    return jnp.dot(a, b, precision=HIGHEST, preferred_element_type=jnp.float32)


def vmem():
    return pl.BlockSpec(memory_space=pltpu.VMEM)


def smem():
    return pl.BlockSpec(memory_space=pltpu.SMEM)


def gather_kernel(rank, pivots, m, o, listed):
    nb, height = o.shape[0], m.shape[0]
    start = rank[0] * height

    def group(g, found):
        for i in range(8):
            k = g * 8 + i
            d = pivots[k] - start
            ours = (d >= 0) & (d < height)
            o[pl.ds(k, 1), :] = m[pl.ds(jnp.where(ours, d, k), 1), :]
            listed[found] = k
            found += (ours & (pivots[k] >= nb)).astype(jnp.int32)
        return found

    listed[nb] = lax.fori_loop(0, nb // 8, group, 0)


def move_rows(rank, pivots, listed, nb, u, o):
    start = rank[0] * o.shape[0]

    def one(i, c):
        k = listed[i]
        o[pl.ds(pivots[k] - start, 1), :] = u[pl.ds(k, 1), :]
        return c

    lax.fori_loop(0, listed[nb], one, 0)


def scatter_kernel(rank, pivots, listed, m, u, o):
    o[...] = m[...]
    move_rows(rank, pivots, listed, u.shape[0], u, o)


def invert_blocks(diag):
    n = BLOCK
    row = lax.broadcasted_iota(jnp.int32, (n, n), 0)
    col = lax.broadcasted_iota(jnp.int32, (n, n), 1)
    eye = jnp.where(row == col, 1.0, 0.0)
    inv = None
    s = 1
    while s < n:
        mask = (row // (2 * s) == col // (2 * s)) & ((row // s) % 2 == 1) & ((col // s) % 2 == 0)
        low = [jnp.where(mask, d, 0.0) for d in diag]
        if inv is None:
            inv = [eye - c for c in low]
        else:
            right = [fdot(c, d) for c, d in zip(low, inv)]
            inv = [d - fdot(d, t) for d, t in zip(inv, right)]
        s *= 2
    return inv


def invert_kernel(u, o):
    n = BLOCK
    count = u.shape[0] // n
    inv = invert_blocks([u[b * n : (b + 1) * n, b * n : (b + 1) * n] for b in range(count)])
    for b in range(count):
        o[b * n : (b + 1) * n, :] = inv[b]


def blocks_below(b):
    return b * (b - 1) // 2


def pack_kernel(rows, stride, blk, at, *refs):
    *bufs, panel, diag, off, sems = refs
    n = BLOCK
    per = rows // n

    def moves(src, base, which):
        for i in range(per):
            b = which * per + i
            for k in range(b + 1):
                part = src.at[pl.ds(base + i * n, n), pl.ds(k * n, n)]
                at_row = (b if k == b else blocks_below(b) + k) * n
                to = (diag if k == b else off).at[pl.ds(at_row, n), :]
                yield pltpu.make_async_copy(part, to, sems.at[blocks_below(b + 1) + k])

    def each(do):
        for i, buf in enumerate(bufs):
            block = blk[i * stride + at[0]]
            for which in range(2):
                if which and buf.shape[1] < 2 * rows:
                    continue

                @pl.when(block == which)
                def _(buf=buf, which=which):
                    for copy in moves(buf, 0, which):
                        do(copy)

        @pl.when(blk[len(bufs) * stride + at[0]] == 0)
        def _():
            for which in range(2):
                for copy in moves(panel, which * rows, which):
                    do(copy)

    each(lambda copy: copy.start())
    each(lambda copy: copy.wait())


def take_by_rank(rank, own, far, near, to, sem, do):
    @pl.when(rank[0] == 0)
    def _():
        do(pltpu.make_async_copy(own, to, sem))

    @pl.when(rank[0] == 2)
    def _():
        do(pltpu.make_async_copy(far, to, sem))

    @pl.when(rank[0] % 2 == 1)
    def _():
        do(pltpu.make_async_copy(near, to, sem))


def invert_diag_kernel(rank, own, far, near, o, u, sem):
    take_by_rank(rank, own, far, near, u, sem, lambda copy: copy.start())
    take_by_rank(rank, own, far, near, u, sem, lambda copy: copy.wait())
    n = BLOCK
    count = u.shape[0] // n
    inv = invert_blocks([u[b * n : (b + 1) * n, :] for b in range(count)])
    for b in range(count):
        o[b * n : (b + 1) * n, :] = inv[b]


def fetch_kernel(rows, want, stride, blk, at, *refs):
    *bufs, panel, o, sem = refs
    for i, buf in enumerate(bufs):

        @pl.when(blk[i * stride + at[0]] == want)
        def _(buf=buf):
            copy = pltpu.make_async_copy(buf.at[pl.ds(0, rows), :], o, sem)
            copy.start()
            copy.wait()

    @pl.when(blk[len(bufs) * stride + at[0]] == 0)
    def _():
        copy = pltpu.make_async_copy(panel.at[pl.ds(want * rows, rows), :], o, sem)
        copy.start()
        copy.wait()


def split_kernel(rows, carrier, stride, blk, at, *refs):
    *bufs, panel, weights, o, sums, stage, sems, more = refs
    total = panel.shape[0]

    def copies(do):
        for i, buf in enumerate(bufs):
            block = blk[i * stride + at[0]]

            @pl.when(block >= 0)
            def _(i=i, buf=buf, block=block):
                place = pl.ds(pl.multiple_of(block * rows, rows), rows)
                do(pltpu.make_async_copy(buf.at[pl.ds(0, rows), :], stage.at[place, :], sems.at[i]))

            if carrier is not None:

                @pl.when(block == carrier)
                def _(i=i, buf=buf):
                    do(pltpu.make_async_copy(buf.at[pl.ds(rows, 8), :], sums, more.at[i]))

        @pl.when(blk[len(bufs) * stride + at[0]] == 0)
        def _():
            do(pltpu.make_async_copy(panel, stage, sems.at[len(bufs)]))
            if carrier is not None:
                do(pltpu.make_async_copy(weights, sums, more.at[len(bufs)]))

        if carrier is None:
            do(pltpu.make_async_copy(weights, sums, more.at[len(bufs)]))

    copies(lambda copy: copy.start())
    copies(lambda copy: copy.wait())
    n = BLOCK
    for r in range(0, total, n):
        for k in range(panel.shape[1] // n):
            o[r : r + n, 3 * n * k : 3 * n * (k + 1)] = wide(stage[r : r + n, k * n : (k + 1) * n])


def wide(x):
    hi, lo = split(x)
    return jnp.concatenate([hi, hi, lo], axis=1)


def tall(x):
    hi, lo = split(x)
    return jnp.concatenate([hi, lo, hi], axis=0)


def final_kernel(scale, strip, flag, p, u, inv, ll_in, w, sw_in, ck, o, nc, s3, uu, ii, ob, ll, sw, got, sent):
    arrivals = [pltpu.make_async_copy(ll_in, ll, got.at[0]), pltpu.make_async_copy(sw_in, sw, got.at[1])]
    for copy in arrivals:
        copy.start()
    nb, cols = p.shape
    n = BLOCK
    count = nb // n
    for b in range(count):
        rows = slice(b * n, (b + 1) * n)
        ii[rows, :] = wide(inv[rows, :])
        for k in range(b):
            uu[rows, 3 * n * k : 3 * n * (k + 1)] = wide(u[rows, k * n : (k + 1) * n])
    for b in range(count):
        rows = slice(b * n, (b + 1) * n)
        for c in range(0, cols, strip):
            at = slice(c, c + strip)
            x = p[rows, at]
            if b:
                x = x - bdot(uu[rows, : 3 * n * b], s3[: 3 * n * b, at])
            solved = bdot(ii[rows, :], tall(x))
            s3[3 * n * b : 3 * n * (b + 1), at] = tall(solved)
            ob[rows, at] = solved
    for copy in arrivals:
        copy.wait()
    wrows = jnp.concatenate([wide(w[:, k * n : (k + 1) * n]) for k in range(count)], axis=1)
    is_top = flag[0] == 1
    leaving = []
    for c in range(0, cols, strip):
        at = slice(c, c + strip)
        sums = jnp.sum(p[:, at] - ob[:nb, at], 0, keepdims=True) + bdot(wrows, s3[:, at])[0:1, :]
        nc[:, at] = ck[:, at] - sums * scale
        for r in range(0, sw.shape[0], nb):
            rows = slice(r, r + nb)
            value = sw[rows, at] - bdot(ll[rows, :], s3[:, at])
            if r == 0:
                value = jnp.where(is_top, ob[rows, at], value)
            ob[rows, at] = value
            copy = pltpu.make_async_copy(ob.at[rows, at], o.at[rows, at], sent.at[len(leaving)])
            copy.start()
            leaving.append(copy)
    for copy in leaving:
        copy.wait()


def finish_kernel(scale, strip, rows, carrier, stride, count, rank, pivots, listed, blk, at, which, inv, ck, *refs):
    bufs, (panel, weights, x, base, near, far, m, u0, u2, u1) = refs[:count], refs[count : count + 10]
    o, nc, picked, core, full, stage, ll, w, sw, s3, uu, ii, ob, u, sems, lsem, wsem, sent = refs[count + 10 :]
    nb, half = full.shape[0], near.shape[0]
    n, cols = BLOCK, picked.shape[1]
    blocks = nb // n
    mine = pl.multiple_of((rank[0] % 2) * half, half)
    theirs = pl.multiple_of(half - mine, half)
    loads = []
    for b in range(blocks):
        rs = pl.ds(b * n, n)
        group = [(x.at[rs, :], picked.at[rs, :]), (base.at[rs, :], core.at[rs, :])]
        if b * n < half:
            group.append((near.at[rs, :], full.at[pl.ds(mine + b * n, n), :]))
            group.append((far.at[rs, :], full.at[pl.ds(theirs + b * n, n), :]))
        loads.append([pltpu.make_async_copy(src, to, sems.at[4 * b + i]) for i, (src, to) in enumerate(group)])
    whole = pltpu.make_async_copy(m, sw, sems.at[4 * blocks])
    last = sems.at[4 * blocks + 1]

    def pieces(do):
        for i, buf in enumerate(bufs):
            block = blk[i * stride + at[0]]

            @pl.when(block >= 0)
            def _(i=i, buf=buf, block=block):
                place = pl.ds(pl.multiple_of(block * rows, rows), rows)
                do(pltpu.make_async_copy(buf.at[pl.ds(0, rows), :], stage.at[place, :], lsem.at[i]))

            @pl.when(block == carrier)
            def _(i=i, buf=buf):
                do(pltpu.make_async_copy(buf.at[pl.ds(rows, 8), :], w, wsem.at[i]))

        @pl.when(blk[count * stride + at[0]] == 0)
        def _():
            do(pltpu.make_async_copy(panel, stage, lsem.at[count]))
            do(pltpu.make_async_copy(weights, w, wsem.at[count]))

    take_by_rank(rank, u0, u2, u1, u, last, lambda copy: copy.start())
    for group in loads:
        for copy in group:
            copy.start()
    pieces(lambda copy: copy.start())
    whole.start()
    for b in range(blocks):
        ii[b * n : (b + 1) * n, :] = wide(inv[b * n : (b + 1) * n, :])
    take_by_rank(rank, u0, u2, u1, u, last, lambda copy: copy.wait())
    for b in range(blocks):
        for k in range(b):
            r = (blocks_below(b) + k) * n
            uu[b * n : (b + 1) * n, 3 * n * k : 3 * n * (k + 1)] = wide(u[r : r + n, :])
    for b in range(blocks):
        for copy in loads[b]:
            copy.wait()
        r = slice(b * n, (b + 1) * n)
        pick = which[r, :]
        for c in range(0, cols, strip):
            cs = slice(c, c + strip)
            p = jnp.where(pick == 2, full[r, cs], jnp.where(pick == 1, core[r, cs], picked[r, cs]))
            picked[r, cs] = p
            if b:
                p = p - bdot(uu[r, : 3 * n * b], s3[: 3 * n * b, cs])
            solved = bdot(ii[r, :], tall(p))
            s3[3 * n * b : 3 * n * (b + 1), cs] = tall(solved)
            ob[r, cs] = solved
    whole.wait()

    @pl.when(rank[0] == 0)
    def _():
        move_rows(rank, pivots, listed, nb, sw, sw)

    @pl.when(rank[0] == 1)
    def _():
        move_rows(rank, pivots, listed, nb, core, sw)

    @pl.when(rank[0] >= 2)
    def _():
        move_rows(rank, pivots, listed, nb, full, sw)

    pieces(lambda copy: copy.wait())
    for r in range(0, sw.shape[0], n):
        for k in range(blocks):
            ll[r : r + n, 3 * n * k : 3 * n * (k + 1)] = wide(stage[r : r + n, k * n : (k + 1) * n])
    wrows = jnp.concatenate([wide(w[:, k * n : (k + 1) * n]) for k in range(blocks)], axis=1)
    is_top = rank[0] == 0
    leaving = []
    for c in range(0, cols, strip):
        cs = slice(c, c + strip)
        sums = jnp.sum(picked[:, cs] - ob[:nb, cs], 0, keepdims=True) + bdot(wrows, s3[:, cs])[0:1, :]
        nc[cs] = ck[cs] - (sums * scale).reshape(strip)
        for r in range(0, sw.shape[0], nb):
            rs = slice(r, r + nb)
            value = sw[rs, cs] - bdot(ll[rs, :], s3[:, cs])
            if r == 0:
                value = jnp.where(is_top, ob[rs, cs], value)
            ob[rs, cs] = value
            copy = pltpu.make_async_copy(ob.at[rs, cs], o.at[rs, cs], sent.at[len(leaving)])
            copy.start()
            leaving.append(copy)
    for copy in leaving:
        copy.wait()


def stream(panel, n_col, chunks, lag):
    depth = n_col // 2
    col = lax.axis_index("col")
    is_root, is_side = col == 0, col == 1
    n = panel.shape[0] // (2 * chunks)
    a = [panel[2 * j * n : (2 * j + 1) * n] for j in range(chunks)]
    b = [panel[(2 * j + 1) * n : (2 * j + 2) * n] for j in range(chunks)]
    z, y = col // 2, col % 2
    along, across = {}, {}
    blocks = {}
    for t in range(max(chunks + lag * depth, 2 * chunks)):
        z_pairs, y_pairs = [], []
        for zz in range(depth):
            for yy in range(2):
                j = t - lag * zz - lag * yy
                if 0 <= j < chunks:
                    if zz < depth - 1:
                        z_pairs.append((2 * zz + yy, 2 * zz + 2 + yy))
                    if zz > 0:
                        y_pairs.append((2 * zz + yy, 2 * zz + 1 - yy))
        if t < 2 * chunks:
            y_pairs.append((0, 1))
        before_z, before_y = along.get(t - lag), across.get(t - lag)
        if t < chunks:
            z_in = b[t] if before_z is None else jnp.where(is_root, b[t], before_z)
        else:
            z_in = before_z
        if z_in is not None and before_y is not None:
            z_in = jnp.where(is_side, before_y, z_in)
        head = a[t] if t < chunks else (b[t - chunks] if t < 2 * chunks else None)
        if head is None:
            y_in = z_in
        elif z_in is None:
            y_in = head
        else:
            y_in = jnp.where(is_root, head, z_in)
        if y_pairs:
            across[t] = lax.ppermute(y_in, "col", y_pairs)
            j = t - lag * z - lag * (1 - y)
            ok = (z > 0) & (j >= 0) & (j < chunks)
            value = jnp.where(ok, 2 * j + y, -1)
            if t < 2 * chunks:
                first = 2 * t if t < chunks else 2 * (t - chunks) + 1
                value = jnp.where(is_side, first, value)
            blocks["y", t] = value
        if z_pairs:
            along[t] = lax.ppermute(z_in, "col", z_pairs)
            j = t - lag * (z - 1) - lag * y
            ok = (z > 0) & (j >= 0) & (j < chunks)
            blocks["z", t] = jnp.where(ok, 2 * j + 1 - y, -1)
    return n, along, across, blocks, is_root


def anyspace():
    return pl.BlockSpec(memory_space=pl.ANY)


def fetch(found, rows, want):
    blk, at, stride, bufs = found
    return pl.pallas_call(
        functools.partial(fetch_kernel, rows, want, stride),
        out_shape=jax.ShapeDtypeStruct((rows, bufs[0].shape[1]), jnp.float32),
        in_specs=[smem()] * 2 + [anyspace()] * len(bufs),
        out_specs=vmem(),
        scratch_shapes=[pltpu.SemaphoreType.DMA],
        cost_estimate=pl.CostEstimate(flops=0, bytes_accessed=8 * bufs[0].size, transcendentals=0),
    )(blk, at, *bufs)


def split_panel(found, rows, carrier, weights):
    blk, at, stride, bufs = found
    panel = bufs[-1]
    return pl.pallas_call(
        functools.partial(split_kernel, rows, carrier, stride),
        out_shape=(
            jax.ShapeDtypeStruct((panel.shape[0], 3 * panel.shape[1]), jnp.bfloat16),
            jax.ShapeDtypeStruct(weights.shape, jnp.float32),
        ),
        in_specs=[smem()] * 2 + [anyspace()] * (len(bufs) + 1),
        out_specs=(vmem(), vmem()),
        scratch_shapes=[
            pltpu.VMEM(panel.shape, jnp.float32),
            pltpu.SemaphoreType.DMA((len(bufs),)),
            pltpu.SemaphoreType.DMA((len(bufs),)),
        ],
        cost_estimate=pl.CostEstimate(flops=0, bytes_accessed=10 * panel.size, transcendentals=0),
    )(blk, at, *bufs, weights)


def halves(own, other, high):
    return jnp.concatenate(
        [jnp.where(high, other, own), jnp.where(high, own, other)], axis=0
    )


def one(value):
    return value.astype(jnp.int32)[None]


def scatter_rows(row, pivots, listed, matrix, upper):
    return pl.pallas_call(
        scatter_kernel,
        out_shape=jax.ShapeDtypeStruct(matrix.shape, jnp.float32),
        in_specs=[smem(), smem(), smem(), vmem(), vmem()],
        out_specs=vmem(),
        cost_estimate=pl.CostEstimate(flops=0, bytes_accessed=8 * matrix.size, transcendentals=0),
    )(one(row), pivots, listed, matrix, upper)


def gather_rows(row, pivots, matrix):
    nb = pivots.shape[0]
    return pl.pallas_call(
        gather_kernel,
        out_shape=(
            jax.ShapeDtypeStruct((nb, matrix.shape[1]), jnp.float32),
            jax.ShapeDtypeStruct((nb + 8,), jnp.int32),
        ),
        in_specs=[smem(), smem(), vmem()],
        out_specs=(vmem(), smem()),
        cost_estimate=pl.CostEstimate(flops=0, bytes_accessed=8 * matrix.size, transcendentals=0),
    )(one(row), pivots, matrix)


def panel_sums(panel, row, nb):
    local_rows = panel.shape[0]
    global_rows = row * local_rows + jnp.arange(local_rows, dtype=jnp.int32)
    sums = jnp.sum(jnp.where((global_rows >= nb)[:, None], panel, 0.0), 0, keepdims=True)
    return jnp.broadcast_to(sums, (8, nb))


def exchange(panel, matrix, pivots):
    nb = pivots.shape[0]
    local_rows = matrix.shape[0]
    n_row, n_col = lax.axis_size("row"), lax.axis_size("col")
    row, col = lax.axis_index("row"), lax.axis_index("col")
    high = (row % 2) == 1
    owner = pivots // local_rows
    rows, along, across, blocks, is_root = stream(panel, n_col, CHUNKS, LAG)
    weights = panel_sums(panel, row, nb)
    bit = 1
    while bit < n_row:
        weights += lax.ppermute(weights, "row", [(i, i ^ bit) for i in range(n_row)])
        bit *= 2
    bit = 1
    while bit < n_col:
        moved = lax.ppermute(weights, "col", [(i, i + bit) for i in range(bit)])
        weights = jnp.where((col >= bit) & (col < 2 * bit), moved, weights)
        bit *= 2
    picked, listed = gather_rows(row, pivots, matrix)
    upper = matrix[:nb]
    half = nb // 2
    swap_all = [(i, i ^ 1) for i in range(n_row)]
    bit, level = 1, 0
    while bit < n_row:
        pairs = [(i, i ^ bit) for i in range(n_row)]
        if bit == 1:
            other = lax.ppermute(picked, "row", pairs)
        else:
            piece = lax.dynamic_slice_in_dim(picked, jnp.where(high, half, 0), half, 0)
            piece = lax.ppermute(piece, "row", pairs)
            other = halves(piece, lax.ppermute(piece, "row", swap_all), high)
        group = row >> level
        upper = jnp.where(group == 1, other, upper)
        theirs = (owner >> level) == (group ^ 1)
        outside = (owner >> level) != group
        picked = jnp.where((theirs | (outside & (group == 1)))[:, None], other, picked)
        bit, level = 2 * bit, level + 1
    blk = jnp.stack(list(blocks.values()) + [jnp.where(is_root, 0, -1)]).astype(jnp.int32)
    bufs = [(across if kind == "y" else along)[t] for kind, t in blocks] + [panel]
    found = blk, jnp.zeros((1,), jnp.int32), 1, bufs
    diag = jnp.concatenate([fetch(found, rows, b) for b in range(nb // rows)], 0)
    moved = lax.ppermute(diag, "row", [(0, 1)])
    diag = jnp.where(row == 1, moved, diag)
    bit = 2
    while bit < n_row:
        piece = lax.dynamic_slice_in_dim(diag, jnp.where(high, half, 0), half, 0)
        piece = lax.ppermute(piece, "row", [(i, i + bit) for i in range(bit)])
        other = lax.ppermute(piece, "row", [(i, i ^ 1) for i in range(bit, 2 * bit)])
        diag = jnp.where((row >= bit) & (row < 2 * bit), halves(piece, other, high), diag)
        bit *= 2
    swapped = scatter_rows(row, pivots, listed, matrix, upper)
    return (found, rows, None, weights), picked, swapped, diag


def fence(*values):
    return lax.optimization_barrier(values)


def step_4x8(panel, matrix, pivots, checks):
    nb = pivots.shape[0]
    local_rows = matrix.shape[0]
    row, col = lax.axis_index("row"), lax.axis_index("col")
    z = col // 2
    high = (row % 2) == 1
    is_root, is_side = col == 0, col == 1
    n = local_rows // 4
    at = lambda zz, yy: 2 * zz + yy
    owner = pivots // local_rows
    half = nb // 2
    in_pair = (owner >> 1) == (row >> 1)
    from_core = (owner == (row ^ 1)) | (~in_pair & (row == 1))
    which = jnp.where(in_pair, jnp.where(owner == row, 0, 1), 2).astype(jnp.int32)[:, None]
    core = [(i, i ^ 1) for i in range(4)]
    across_x = [(i, i ^ 2) for i in range(4)]
    send = lambda x, pairs: lax.ppermute(x, "row", pairs)
    r, s = at(0, 0), at(0, 1)
    plan_dn = [
        [(r, at(2, 0), 1)],
        [(r, at(2, 0), 3), (s, at(2, 1), 0), (at(2, 0), at(1, 0), 1)],
        [(r, at(2, 0), 2), (s, at(2, 1), 2), (at(2, 0), at(1, 0), 3), (at(2, 1), at(1, 1), 0)],
        [(at(2, 0), at(1, 0), 2), (at(2, 1), at(1, 1), 2)],
    ]
    plan_n3 = [
        [],
        [(at(2, 0), at(3, 0), 1)],
        [(at(2, 0), at(3, 0), 3), (at(2, 1), at(3, 1), 0)],
        [(at(2, 0), at(3, 0), 2), (at(2, 1), at(3, 1), 2)],
    ]
    plan_y = [
        [(r, s, 0)],
        [(r, s, 2), (at(2, 0), at(2, 1), 1)],
        [(r, s, 1), (at(2, 0), at(2, 1), 3), (at(2, 1), at(2, 0), 0)]
        + [(at(zz, 0), at(zz, 1), 1) for zz in (1, 3)],
        [(r, s, 3)]
        + [(at(zz, 0), at(zz, 1), 3) for zz in (1, 3)]
        + [(at(zz, 1), at(zz, 0), 0) for zz in (1, 3)],
    ]
    root_v, root_w = [1, 3, 2, None], [0, 2, 1, 3]
    dn, n3, ys = {}, {}, {}
    order, table = [], []

    def move(value, plan, kind, t):
        order.append((kind, t))
        line = [-1] * 8
        for _, target, block in plan:
            line[target] = block
        table.append(line)
        return lax.ppermute(value, "col", [(a, b) for a, b, _ in plan])

    def have(last):
        made = {"dn": dn, "n3": n3, "y": ys}
        keys = [i for i, (_, t) in enumerate(order) if t <= last]
        lines = jnp.asarray([table[i] for i in keys] + [[0] + [-1] * 7], jnp.int32)
        bufs = [made[order[i][0]][order[i][1]] for i in keys] + [panel]
        return lines.reshape(-1), one(col), 8, bufs

    def quarter(i):
        rows = source[i * n : (i + 1) * n]
        return jnp.concatenate([rows, weights if i == 2 else jnp.zeros_like(weights)], 0)

    source = panel
    tri = panel[:n, :half]
    everyone = ("row", "col")
    for t in range(4):
        if t == 0:
            weights = jnp.zeros((8, nb), jnp.float32)
            v = quarter(1)
            (source,) = fence(panel)
            w = quarter(0)
        else:
            v = dn[t - 1] if t == 3 else jnp.where(is_side, ys[t - 1], dn[t - 1])
            if root_v[t] is not None:
                v = jnp.where(is_root, quarter(root_v[t]), v)
            from_dn, source, weights = fence(dn[t - 1], source, weights)
            w = jnp.where(z == 3, n3[t - 1], from_dn) if t > 1 else from_dn
            w = jnp.where(is_root, quarter(root_w[t]), w)
        dn[t] = move(v, plan_dn[t], "dn", t)
        if plan_n3[t]:
            n3[t] = move(v, plan_n3[t], "n3", t)
        ys[t] = move(w, plan_y[t], "y", t)
        extra = []
        if t == 0:
            weights = panel_sums(panel, row, nb)
            for bit in (1, 2):
                weights += send(weights, [(i, i ^ bit) for i in range(4)])
            picked, listed = gather_rows(row, pivots, matrix)
            base = send(picked, core)
            extra = [source]
        if t == 1:
            first = jnp.where(high, half, 0)
            cut = lambda x: lax.dynamic_slice_in_dim(x, first, half, 0)
            piece = jnp.where(cut(from_core[:, None]), cut(base), cut(picked))
            near = send(piece, across_x)
            tri1 = lax.ppermute(tri, everyone, [(r, at(1, 0))])
            tri3 = lax.ppermute(tri, everyone, [(r, at(3, 0))])
        if t == 2:
            extra = [tri1, tri3]
        groups = [d for d in (dn, n3, ys) if t in d]
        if t < 3:
            fenced = list(fence(*[d[t] for d in groups], *extra))
            for d in groups:
                d[t] = fenced.pop(0)
            if t == 0:
                (source,) = fenced
            elif t == 2:
                tri1, tri3 = fenced
    lines, where, stride, bufs = have(2)
    lines = jnp.concatenate([lines[:-8], jnp.asarray([-1] * 16 + [0] + [-1] * 7, jnp.int32)])
    lines = lines.at[len(bufs) * 8 - 8 + at(1, 0)].set(0).at[len(bufs) * 8 + at(3, 0)].set(0)
    below = nb // BLOCK * (nb // BLOCK - 1) // 2 * BLOCK
    diag, off = pl.pallas_call(
        functools.partial(pack_kernel, n, stride),
        out_shape=(
            jax.ShapeDtypeStruct((nb, BLOCK), jnp.float32),
            jax.ShapeDtypeStruct((below, BLOCK), jnp.float32),
        ),
        in_specs=[smem()] * 2 + [anyspace()] * (len(bufs) + 2),
        out_specs=(vmem(), vmem()),
        scratch_shapes=[pltpu.SemaphoreType.DMA((nb // BLOCK * (nb // BLOCK + 1) // 2,))],
        cost_estimate=pl.CostEstimate(flops=0, bytes_accessed=8 * n * nb, transcendentals=0),
    )(lines, where, *bufs[:-1], tri1, tri3, panel)
    far_diag = send(diag, [(0, 2)])
    far_off = send(off, [(0, 2)])
    other = send(near, core)
    close_diag = send(jnp.where(row == 2, far_diag, diag), [(0, 1), (2, 3)])
    inverse = pl.pallas_call(
        invert_diag_kernel,
        out_shape=jax.ShapeDtypeStruct((nb, BLOCK), jnp.float32),
        in_specs=[smem()] + [anyspace()] * 3,
        out_specs=vmem(),
        scratch_shapes=[pltpu.VMEM((nb, BLOCK), jnp.float32), pltpu.SemaphoreType.DMA],
        cost_estimate=pl.CostEstimate(flops=10**9, bytes_accessed=nb * nb * 4, transcendentals=0),
    )(one(row), diag, far_diag, close_diag)
    close_off = send(jnp.where(row == 2, far_off, off), [(0, 1), (2, 3)])
    lines, where, stride, bufs = have(3)
    cols = matrix.shape[1]
    strip = 256 if cols % 256 == 0 else cols
    count = len(bufs) - 1
    bf, f32 = jnp.bfloat16, jnp.float32
    return pl.pallas_call(
        functools.partial(
            finish_kernel, 1.0 / float((local_rows * 4) ** 0.5), strip, n, 2, stride, count
        ),
        out_shape=(
            jax.ShapeDtypeStruct(matrix.shape, f32),
            jax.ShapeDtypeStruct((cols,), f32),
        ),
        in_specs=[smem()] * 5 + [vmem()] * 3 + [anyspace()] * (count + 10),
        out_specs=(anyspace(), vmem()),
        scratch_shapes=[
            pltpu.VMEM((nb, cols), f32),
            pltpu.VMEM((nb, cols), f32),
            pltpu.VMEM((nb, cols), f32),
            pltpu.VMEM(panel.shape, f32),
            pltpu.VMEM((local_rows, 3 * nb), bf),
            pltpu.VMEM((8, nb), f32),
            pltpu.VMEM(matrix.shape, f32),
            pltpu.VMEM((3 * nb, cols), bf),
            pltpu.VMEM((nb, 3 * nb), bf),
            pltpu.VMEM((nb, 3 * BLOCK), bf),
            pltpu.VMEM(matrix.shape, f32),
            pltpu.VMEM(off.shape, f32),
            pltpu.SemaphoreType.DMA((4 * (nb // BLOCK) + 2,)),
            pltpu.SemaphoreType.DMA((count + 1,)),
            pltpu.SemaphoreType.DMA((count + 1,)),
            pltpu.SemaphoreType.DMA((cols // strip * (local_rows // nb),)),
        ],
    )(
        one(row), pivots, listed, lines, where, which, inverse, checks,
        *bufs[:-1], panel, weights, picked, base, near, other, matrix, off, far_off, close_off,
    )


def local(matrix, panel_lower, pivots, checks):
    local_rows, local_cols = matrix.shape
    nb = pivots.shape[0]
    n_row, n_col = lax.axis_size("row"), lax.axis_size("col")
    row = lax.axis_index("row")
    special = n_row == 4 and n_col == 8 and nb == local_rows // 2
    if special:
        return step_4x8(panel_lower[0], matrix, pivots, checks)
    pieces, picked, swapped, diag = exchange(panel_lower[0], matrix, pivots)
    inverse = pl.pallas_call(
        invert_kernel,
        out_shape=jax.ShapeDtypeStruct((nb, BLOCK), jnp.float32),
        in_specs=[vmem()],
        out_specs=vmem(),
        cost_estimate=pl.CostEstimate(flops=10**9, bytes_accessed=nb * nb * 4, transcendentals=0),
    )(diag)
    lower, weights = split_panel(*pieces)
    strip = 256 if local_cols % 256 == 0 else local_cols
    scale = 1.0 / float((local_rows * n_row) ** 0.5)
    bf = jnp.bfloat16
    updated, new_checks = pl.pallas_call(
        functools.partial(final_kernel, scale, strip),
        out_shape=(
            jax.ShapeDtypeStruct(matrix.shape, jnp.float32),
            jax.ShapeDtypeStruct((1, local_cols), jnp.float32),
        ),
        in_specs=[smem()] + [vmem()] * 3 + [anyspace(), vmem(), anyspace(), vmem()],
        out_specs=(anyspace(), vmem()),
        scratch_shapes=[
            pltpu.VMEM((3 * nb, local_cols), bf),
            pltpu.VMEM((nb, 3 * nb), bf),
            pltpu.VMEM((nb, 3 * BLOCK), bf),
            pltpu.VMEM(matrix.shape, jnp.float32),
            pltpu.VMEM(lower.shape, bf),
            pltpu.VMEM(matrix.shape, jnp.float32),
            pltpu.SemaphoreType.DMA((2,)),
            pltpu.SemaphoreType.DMA((local_cols // strip * (local_rows // nb),)),
        ],
    )(
        jnp.where(row == 0, 1, 0).astype(jnp.int32)[None],
        picked,
        diag,
        inverse,
        lower,
        weights,
        swapped,
        checks[None, :],
    )
    return updated, new_checks[0]


def solution(mesh):
    return jax.shard_map(
        local,
        mesh=mesh,
        in_specs=(P("row", "col"), P("col", "row", None), P(), P("col")),
        out_specs=(P("row", "col"), P("col")),
        check_vma=False,
    )
```

```python
import functools

import jax
import jax.numpy as jnp
from jax import lax
from jax.experimental import pallas as pl
from jax.experimental.pallas import tpu as pltpu
from jax.sharding import PartitionSpec as P


BLOCK = 128
CHUNKS = 4
LAG = 1
HIGHEST = lax.Precision.HIGHEST


def split(x):
    hi = x.astype(jnp.bfloat16)
    return hi, (x - hi.astype(jnp.float32)).astype(jnp.bfloat16)


def bdot(a, b):
    return jnp.dot(a, b, preferred_element_type=jnp.float32)


def fdot(a, b):
    return jnp.dot(a, b, precision=HIGHEST, preferred_element_type=jnp.float32)


def vmem():
    return pl.BlockSpec(memory_space=pltpu.VMEM)


def smem():
    return pl.BlockSpec(memory_space=pltpu.SMEM)


def gather_kernel(rank, pivots, m, o, listed):
    nb, height = o.shape[0], m.shape[0]
    start = rank[0] * height

    def group(g, found):
        for i in range(8):
            k = g * 8 + i
            d = pivots[k] - start
            ours = (d >= 0) & (d < height)
            o[pl.ds(k, 1), :] = m[pl.ds(jnp.where(ours, d, k), 1), :]
            listed[found] = k
            found += (ours & (pivots[k] >= nb)).astype(jnp.int32)
        return found

    listed[nb] = lax.fori_loop(0, nb // 8, group, 0)


def move_rows(rank, pivots, listed, nb, u, o):
    start = rank[0] * o.shape[0]

    def one(i, c):
        k = listed[i]
        o[pl.ds(pivots[k] - start, 1), :] = u[pl.ds(k, 1), :]
        return c

    lax.fori_loop(0, listed[nb], one, 0)


def scatter_kernel(rank, pivots, listed, m, u, o):
    o[...] = m[...]
    move_rows(rank, pivots, listed, u.shape[0], u, o)


def invert_blocks(diag):
    n = BLOCK
    row = lax.broadcasted_iota(jnp.int32, (n, n), 0)
    col = lax.broadcasted_iota(jnp.int32, (n, n), 1)
    eye = jnp.where(row == col, 1.0, 0.0)
    inv = None
    s = 1
    while s < n:
        mask = (row // (2 * s) == col // (2 * s)) & ((row // s) % 2 == 1) & ((col // s) % 2 == 0)
        low = [jnp.where(mask, d, 0.0) for d in diag]
        if inv is None:
            inv = [eye - c for c in low]
        else:
            right = [fdot(c, d) for c, d in zip(low, inv)]
            inv = [d - fdot(d, t) for d, t in zip(inv, right)]
        s *= 2
    return inv


def invert_kernel(u, o):
    n = BLOCK
    count = u.shape[0] // n
    inv = invert_blocks([u[b * n : (b + 1) * n, b * n : (b + 1) * n] for b in range(count)])
    for b in range(count):
        o[b * n : (b + 1) * n, :] = inv[b]


def blocks_below(b):
    return b * (b - 1) // 2


def pack_kernel(rows, stride, blk, at, *refs):
    *bufs, panel, o, sems = refs
    n = BLOCK
    per = rows // n

    def moves(src, base, which):
        for i in range(per):
            b = which * per + i
            for k in range(b + 1):
                part = src.at[pl.ds(base + i * n, n), pl.ds(k * n, n)]
                to = o.at[pl.ds((b if k == b else 2 * per + blocks_below(b) + k) * n, n), :]
                yield pltpu.make_async_copy(part, to, sems.at[blocks_below(b + 1) + k])

    def each(do):
        for i, buf in enumerate(bufs):
            block = blk[i * stride + at[0]]
            for which in range(2):
                if which and buf.shape[1] < 2 * rows:
                    continue

                @pl.when(block == which)
                def _(buf=buf, which=which):
                    for copy in moves(buf, 0, which):
                        do(copy)

        @pl.when(blk[len(bufs) * stride + at[0]] == 0)
        def _():
            for which in range(2):
                for copy in moves(panel, which * rows, which):
                    do(copy)

    each(lambda copy: copy.start())
    each(lambda copy: copy.wait())


def take_by_rank(rank, first, own, far, near, to, sem, do):
    rows = pl.ds(first, to.shape[0])

    @pl.when(rank[0] == 0)
    def _():
        do(pltpu.make_async_copy(own.at[rows, :], to, sem))

    @pl.when(rank[0] == 2)
    def _():
        do(pltpu.make_async_copy(far.at[rows, :], to, sem))

    @pl.when(rank[0] % 2 == 1)
    def _():
        do(pltpu.make_async_copy(near.at[rows, :], to, sem))


def invert_diag_kernel(rank, own, far, near, o, u, sem):
    take_by_rank(rank, 0, own, far, near, u, sem, lambda copy: copy.start())
    take_by_rank(rank, 0, own, far, near, u, sem, lambda copy: copy.wait())
    n = BLOCK
    count = u.shape[0] // n
    inv = invert_blocks([u[b * n : (b + 1) * n, :] for b in range(count)])
    for b in range(count):
        o[b * n : (b + 1) * n, :] = inv[b]


def fetch_kernel(rows, want, stride, blk, at, *refs):
    *bufs, panel, o, sem = refs
    for i, buf in enumerate(bufs):

        @pl.when(blk[i * stride + at[0]] == want)
        def _(buf=buf):
            copy = pltpu.make_async_copy(buf.at[pl.ds(0, rows), :], o, sem)
            copy.start()
            copy.wait()

    @pl.when(blk[len(bufs) * stride + at[0]] == 0)
    def _():
        copy = pltpu.make_async_copy(panel.at[pl.ds(want * rows, rows), :], o, sem)
        copy.start()
        copy.wait()


def split_kernel(rows, carrier, stride, blk, at, *refs):
    *bufs, panel, weights, o, sums, stage, sems, more = refs
    total = panel.shape[0]

    def copies(do):
        for i, buf in enumerate(bufs):
            block = blk[i * stride + at[0]]

            @pl.when(block >= 0)
            def _(i=i, buf=buf, block=block):
                place = pl.ds(pl.multiple_of(block * rows, rows), rows)
                do(pltpu.make_async_copy(buf.at[pl.ds(0, rows), :], stage.at[place, :], sems.at[i]))

            if carrier is not None:

                @pl.when(block == carrier)
                def _(i=i, buf=buf):
                    do(pltpu.make_async_copy(buf.at[pl.ds(rows, 8), :], sums, more.at[i]))

        @pl.when(blk[len(bufs) * stride + at[0]] == 0)
        def _():
            do(pltpu.make_async_copy(panel, stage, sems.at[len(bufs)]))
            if carrier is not None:
                do(pltpu.make_async_copy(weights, sums, more.at[len(bufs)]))

        if carrier is None:
            do(pltpu.make_async_copy(weights, sums, more.at[len(bufs)]))

    copies(lambda copy: copy.start())
    copies(lambda copy: copy.wait())
    n = BLOCK
    for r in range(0, total, n):
        for k in range(panel.shape[1] // n):
            o[r : r + n, 3 * n * k : 3 * n * (k + 1)] = wide(stage[r : r + n, k * n : (k + 1) * n])


def wide(x):
    hi, lo = split(x)
    return jnp.concatenate([hi, hi, lo], axis=1)


def tall(x):
    hi, lo = split(x)
    return jnp.concatenate([hi, lo, hi], axis=0)


def final_kernel(scale, strip, flag, p, u, inv, ll_in, w, sw_in, ck, o, nc, s3, uu, ii, ob, ll, sw, got, sent):
    arrivals = [pltpu.make_async_copy(ll_in, ll, got.at[0]), pltpu.make_async_copy(sw_in, sw, got.at[1])]
    for copy in arrivals:
        copy.start()
    nb, cols = p.shape
    n = BLOCK
    count = nb // n
    for b in range(count):
        rows = slice(b * n, (b + 1) * n)
        ii[rows, :] = wide(inv[rows, :])
        for k in range(b):
            uu[rows, 3 * n * k : 3 * n * (k + 1)] = wide(u[rows, k * n : (k + 1) * n])
    for b in range(count):
        rows = slice(b * n, (b + 1) * n)
        for c in range(0, cols, strip):
            at = slice(c, c + strip)
            x = p[rows, at]
            if b:
                x = x - bdot(uu[rows, : 3 * n * b], s3[: 3 * n * b, at])
            solved = bdot(ii[rows, :], tall(x))
            s3[3 * n * b : 3 * n * (b + 1), at] = tall(solved)
            ob[rows, at] = solved
    for copy in arrivals:
        copy.wait()
    wrows = jnp.concatenate([wide(w[:, k * n : (k + 1) * n]) for k in range(count)], axis=1)
    is_top = flag[0] == 1
    leaving = []
    for c in range(0, cols, strip):
        at = slice(c, c + strip)
        sums = jnp.sum(p[:, at] - ob[:nb, at], 0, keepdims=True) + bdot(wrows, s3[:, at])[0:1, :]
        nc[:, at] = ck[:, at] - sums * scale
        for r in range(0, sw.shape[0], nb):
            rows = slice(r, r + nb)
            value = sw[rows, at] - bdot(ll[rows, :], s3[:, at])
            if r == 0:
                value = jnp.where(is_top, ob[rows, at], value)
            ob[rows, at] = value
            copy = pltpu.make_async_copy(ob.at[rows, at], o.at[rows, at], sent.at[len(leaving)])
            copy.start()
            leaving.append(copy)
    for copy in leaving:
        copy.wait()


def finish_kernel(scale, strip, rows, carrier, stride, count, rank, pivots, listed, blk, at, which, inv, ck, *refs):
    bufs, (panel, weights, x, base, near, far, m, u0, u2, u1) = refs[:count], refs[count : count + 10]
    o, nc, picked, core, full, stage, ll, w, sw, s3, uu, ii, ob, u, sums, sems, lsem, wsem, sent = refs[count + 10 :]
    nb, half = full.shape[0], near.shape[0]
    n, cols = BLOCK, picked.shape[1]
    blocks = nb // n
    mine = pl.multiple_of((rank[0] % 2) * half, half)
    theirs = pl.multiple_of(half - mine, half)
    loads = []
    for b in range(blocks):
        rs = pl.ds(b * n, n)
        group = [(x.at[rs, :], picked.at[rs, :]), (base.at[rs, :], core.at[rs, :])]
        if b * n < half:
            group.append((near.at[rs, :], full.at[pl.ds(mine + b * n, n), :]))
            group.append((far.at[rs, :], full.at[pl.ds(theirs + b * n, n), :]))
        loads.append([pltpu.make_async_copy(src, to, sems.at[4 * b + i]) for i, (src, to) in enumerate(group)])
    whole = pltpu.make_async_copy(m, sw, sems.at[4 * blocks])
    last = sems.at[4 * blocks + 1]

    def pieces(do):
        for i, buf in enumerate(bufs):
            block = blk[i * stride + at[0]]

            @pl.when(block >= 0)
            def _(i=i, buf=buf, block=block):
                place = pl.ds(pl.multiple_of(block * rows, rows), rows)
                do(pltpu.make_async_copy(buf.at[pl.ds(0, rows), :], stage.at[place, :], lsem.at[i]))

            @pl.when(block == carrier)
            def _(i=i, buf=buf):
                do(pltpu.make_async_copy(buf.at[pl.ds(rows, 8), :], w, wsem.at[i]))

        @pl.when(blk[count * stride + at[0]] == 0)
        def _():
            do(pltpu.make_async_copy(panel, stage, lsem.at[count]))
            do(pltpu.make_async_copy(weights, w, wsem.at[count]))

    take_by_rank(rank, nb, u0, u2, u1, u, last, lambda copy: copy.start())
    for group in loads:
        for copy in group:
            copy.start()
    pieces(lambda copy: copy.start())
    whole.start()
    for b in range(blocks):
        ii[b * n : (b + 1) * n, :] = wide(inv[b * n : (b + 1) * n, :])
    take_by_rank(rank, nb, u0, u2, u1, u, last, lambda copy: copy.wait())
    for b in range(blocks):
        for k in range(b):
            r = (blocks_below(b) + k) * n
            uu[b * n : (b + 1) * n, 3 * n * k : 3 * n * (k + 1)] = wide(u[r : r + n, :])
    on_diagonal = lax.broadcasted_iota(jnp.int32, (n, n), 0) == lax.broadcasted_iota(jnp.int32, (n, n), 1)
    for b in range(blocks):
        for copy in loads[b]:
            copy.wait()
        r = slice(b * n, (b + 1) * n)
        lanes = jnp.broadcast_to(which[b : b + 1, :], (n, n))
        pick = jnp.max(jnp.where(on_diagonal, lanes, 0.0), 1, keepdims=True)
        for c in range(0, cols, strip):
            cs = slice(c, c + strip)
            p = jnp.where(pick == 2, full[r, cs], jnp.where(pick == 1, core[r, cs], picked[r, cs]))
            gained = jnp.sum(p, 0, keepdims=True)
            if b:
                p = p - bdot(uu[r, : 3 * n * b], s3[: 3 * n * b, cs])
            solved = bdot(ii[r, :], tall(p))
            s3[3 * n * b : 3 * n * (b + 1), cs] = tall(solved)
            ob[r, cs] = solved
            gained -= jnp.sum(solved, 0, keepdims=True)
            sums[0:1, cs] = gained if b == 0 else sums[0:1, cs] + gained
    whole.wait()

    @pl.when(rank[0] == 0)
    def _():
        move_rows(rank, pivots, listed, nb, sw, sw)

    @pl.when(rank[0] == 1)
    def _():
        move_rows(rank, pivots, listed, nb, core, sw)

    @pl.when(rank[0] >= 2)
    def _():
        move_rows(rank, pivots, listed, nb, full, sw)

    pieces(lambda copy: copy.wait())
    for r in range(0, sw.shape[0], n):
        for k in range(blocks):
            ll[r : r + n, 3 * n * k : 3 * n * (k + 1)] = wide(stage[r : r + n, k * n : (k + 1) * n])
    wrows = jnp.concatenate([wide(w[:, k * n : (k + 1) * n]) for k in range(blocks)], axis=1)
    is_top = rank[0] == 0
    leaving = []
    for c in range(0, cols, strip):
        cs = slice(c, c + strip)
        change = sums[0:1, cs] + bdot(wrows, s3[:, cs])[0:1, :]
        nc[cs] = ck[cs] - (change * scale).reshape(strip)
        for r in range(0, sw.shape[0], nb):
            rs = slice(r, r + nb)
            value = sw[rs, cs] - bdot(ll[rs, :], s3[:, cs])
            if r == 0:
                value = jnp.where(is_top, ob[rs, cs], value)
            ob[rs, cs] = value
            copy = pltpu.make_async_copy(ob.at[rs, cs], o.at[rs, cs], sent.at[len(leaving)])
            copy.start()
            leaving.append(copy)
    for copy in leaving:
        copy.wait()


def stream(panel, n_col, chunks, lag):
    depth = n_col // 2
    col = lax.axis_index("col")
    is_root, is_side = col == 0, col == 1
    n = panel.shape[0] // (2 * chunks)
    a = [panel[2 * j * n : (2 * j + 1) * n] for j in range(chunks)]
    b = [panel[(2 * j + 1) * n : (2 * j + 2) * n] for j in range(chunks)]
    z, y = col // 2, col % 2
    along, across = {}, {}
    blocks = {}
    for t in range(max(chunks + lag * depth, 2 * chunks)):
        z_pairs, y_pairs = [], []
        for zz in range(depth):
            for yy in range(2):
                j = t - lag * zz - lag * yy
                if 0 <= j < chunks:
                    if zz < depth - 1:
                        z_pairs.append((2 * zz + yy, 2 * zz + 2 + yy))
                    if zz > 0:
                        y_pairs.append((2 * zz + yy, 2 * zz + 1 - yy))
        if t < 2 * chunks:
            y_pairs.append((0, 1))
        before_z, before_y = along.get(t - lag), across.get(t - lag)
        if t < chunks:
            z_in = b[t] if before_z is None else jnp.where(is_root, b[t], before_z)
        else:
            z_in = before_z
        if z_in is not None and before_y is not None:
            z_in = jnp.where(is_side, before_y, z_in)
        head = a[t] if t < chunks else (b[t - chunks] if t < 2 * chunks else None)
        if head is None:
            y_in = z_in
        elif z_in is None:
            y_in = head
        else:
            y_in = jnp.where(is_root, head, z_in)
        if y_pairs:
            across[t] = lax.ppermute(y_in, "col", y_pairs)
            j = t - lag * z - lag * (1 - y)
            ok = (z > 0) & (j >= 0) & (j < chunks)
            value = jnp.where(ok, 2 * j + y, -1)
            if t < 2 * chunks:
                first = 2 * t if t < chunks else 2 * (t - chunks) + 1
                value = jnp.where(is_side, first, value)
            blocks["y", t] = value
        if z_pairs:
            along[t] = lax.ppermute(z_in, "col", z_pairs)
            j = t - lag * (z - 1) - lag * y
            ok = (z > 0) & (j >= 0) & (j < chunks)
            blocks["z", t] = jnp.where(ok, 2 * j + 1 - y, -1)
    return n, along, across, blocks, is_root


def anyspace():
    return pl.BlockSpec(memory_space=pl.ANY)


def fetch(found, rows, want):
    blk, at, stride, bufs = found
    return pl.pallas_call(
        functools.partial(fetch_kernel, rows, want, stride),
        out_shape=jax.ShapeDtypeStruct((rows, bufs[0].shape[1]), jnp.float32),
        in_specs=[smem()] * 2 + [anyspace()] * len(bufs),
        out_specs=vmem(),
        scratch_shapes=[pltpu.SemaphoreType.DMA],
        cost_estimate=pl.CostEstimate(flops=0, bytes_accessed=8 * bufs[0].size, transcendentals=0),
    )(blk, at, *bufs)


def split_panel(found, rows, carrier, weights):
    blk, at, stride, bufs = found
    panel = bufs[-1]
    return pl.pallas_call(
        functools.partial(split_kernel, rows, carrier, stride),
        out_shape=(
            jax.ShapeDtypeStruct((panel.shape[0], 3 * panel.shape[1]), jnp.bfloat16),
            jax.ShapeDtypeStruct(weights.shape, jnp.float32),
        ),
        in_specs=[smem()] * 2 + [anyspace()] * (len(bufs) + 1),
        out_specs=(vmem(), vmem()),
        scratch_shapes=[
            pltpu.VMEM(panel.shape, jnp.float32),
            pltpu.SemaphoreType.DMA((len(bufs),)),
            pltpu.SemaphoreType.DMA((len(bufs),)),
        ],
        cost_estimate=pl.CostEstimate(flops=0, bytes_accessed=10 * panel.size, transcendentals=0),
    )(blk, at, *bufs, weights)


def halves(own, other, high):
    return jnp.concatenate(
        [jnp.where(high, other, own), jnp.where(high, own, other)], axis=0
    )


def one(value):
    return value.astype(jnp.int32)[None]


def scatter_rows(row, pivots, listed, matrix, upper):
    return pl.pallas_call(
        scatter_kernel,
        out_shape=jax.ShapeDtypeStruct(matrix.shape, jnp.float32),
        in_specs=[smem(), smem(), smem(), vmem(), vmem()],
        out_specs=vmem(),
        cost_estimate=pl.CostEstimate(flops=0, bytes_accessed=8 * matrix.size, transcendentals=0),
    )(one(row), pivots, listed, matrix, upper)


def gather_rows(row, pivots, matrix):
    nb = pivots.shape[0]
    return pl.pallas_call(
        gather_kernel,
        out_shape=(
            jax.ShapeDtypeStruct((nb, matrix.shape[1]), jnp.float32),
            jax.ShapeDtypeStruct((nb + 8,), jnp.int32),
        ),
        in_specs=[smem(), smem(), vmem()],
        out_specs=(vmem(), smem()),
        cost_estimate=pl.CostEstimate(flops=0, bytes_accessed=8 * matrix.size, transcendentals=0),
    )(one(row), pivots, matrix)


def panel_sums(panel, row, nb):
    local_rows = panel.shape[0]
    global_rows = row * local_rows + jnp.arange(local_rows, dtype=jnp.int32)
    sums = jnp.sum(jnp.where((global_rows >= nb)[:, None], panel, 0.0), 0, keepdims=True)
    return jnp.broadcast_to(sums, (8, nb))


def exchange(panel, matrix, pivots):
    nb = pivots.shape[0]
    local_rows = matrix.shape[0]
    n_row, n_col = lax.axis_size("row"), lax.axis_size("col")
    row, col = lax.axis_index("row"), lax.axis_index("col")
    high = (row % 2) == 1
    owner = pivots // local_rows
    rows, along, across, blocks, is_root = stream(panel, n_col, CHUNKS, LAG)
    weights = panel_sums(panel, row, nb)
    bit = 1
    while bit < n_row:
        weights += lax.ppermute(weights, "row", [(i, i ^ bit) for i in range(n_row)])
        bit *= 2
    bit = 1
    while bit < n_col:
        moved = lax.ppermute(weights, "col", [(i, i + bit) for i in range(bit)])
        weights = jnp.where((col >= bit) & (col < 2 * bit), moved, weights)
        bit *= 2
    picked, listed = gather_rows(row, pivots, matrix)
    upper = matrix[:nb]
    half = nb // 2
    swap_all = [(i, i ^ 1) for i in range(n_row)]
    bit, level = 1, 0
    while bit < n_row:
        pairs = [(i, i ^ bit) for i in range(n_row)]
        if bit == 1:
            other = lax.ppermute(picked, "row", pairs)
        else:
            piece = lax.dynamic_slice_in_dim(picked, jnp.where(high, half, 0), half, 0)
            piece = lax.ppermute(piece, "row", pairs)
            other = halves(piece, lax.ppermute(piece, "row", swap_all), high)
        group = row >> level
        upper = jnp.where(group == 1, other, upper)
        theirs = (owner >> level) == (group ^ 1)
        outside = (owner >> level) != group
        picked = jnp.where((theirs | (outside & (group == 1)))[:, None], other, picked)
        bit, level = 2 * bit, level + 1
    blk = jnp.stack(list(blocks.values()) + [jnp.where(is_root, 0, -1)]).astype(jnp.int32)
    bufs = [(across if kind == "y" else along)[t] for kind, t in blocks] + [panel]
    found = blk, jnp.zeros((1,), jnp.int32), 1, bufs
    diag = jnp.concatenate([fetch(found, rows, b) for b in range(nb // rows)], 0)
    moved = lax.ppermute(diag, "row", [(0, 1)])
    diag = jnp.where(row == 1, moved, diag)
    bit = 2
    while bit < n_row:
        piece = lax.dynamic_slice_in_dim(diag, jnp.where(high, half, 0), half, 0)
        piece = lax.ppermute(piece, "row", [(i, i + bit) for i in range(bit)])
        other = lax.ppermute(piece, "row", [(i, i ^ 1) for i in range(bit, 2 * bit)])
        diag = jnp.where((row >= bit) & (row < 2 * bit), halves(piece, other, high), diag)
        bit *= 2
    swapped = scatter_rows(row, pivots, listed, matrix, upper)
    return (found, rows, None, weights), picked, swapped, diag


def fence(*values):
    return lax.optimization_barrier(values)


def step_4x8(panel, matrix, pivots, checks):
    nb = pivots.shape[0]
    local_rows = matrix.shape[0]
    row, col = lax.axis_index("row"), lax.axis_index("col")
    z = col // 2
    high = (row % 2) == 1
    is_root, is_side = col == 0, col == 1
    n = local_rows // 4
    at = lambda zz, yy: 2 * zz + yy
    owner = pivots // local_rows
    half = nb // 2
    in_pair = (owner >> 1) == (row >> 1)
    from_core = (owner == (row ^ 1)) | (~in_pair & (row == 1))
    which = jnp.where(in_pair, jnp.where(owner == row, 0.0, 1.0), 2.0).reshape(nb // BLOCK, BLOCK)
    core = [(i, i ^ 1) for i in range(4)]
    across_x = [(i, i ^ 2) for i in range(4)]
    send = lambda x, pairs: lax.ppermute(x, "row", pairs)
    r, s = at(0, 0), at(0, 1)
    plan_dn = [
        [(r, at(2, 0), 1)],
        [(r, at(2, 0), 3), (s, at(2, 1), 0), (at(2, 0), at(1, 0), 1)],
        [(r, at(2, 0), 2), (s, at(2, 1), 2), (at(2, 0), at(1, 0), 3), (at(2, 1), at(1, 1), 0)],
        [(at(2, 0), at(1, 0), 2), (at(2, 1), at(1, 1), 2)],
    ]
    plan_n3 = [
        [],
        [(at(2, 0), at(3, 0), 1)],
        [(at(2, 0), at(3, 0), 3), (at(2, 1), at(3, 1), 0)],
        [(at(2, 0), at(3, 0), 2), (at(2, 1), at(3, 1), 2)],
    ]
    plan_y = [
        [(r, s, 0)],
        [(r, s, 2), (at(2, 0), at(2, 1), 1)],
        [(r, s, 1), (at(2, 0), at(2, 1), 3), (at(2, 1), at(2, 0), 0)]
        + [(at(zz, 0), at(zz, 1), 1) for zz in (1, 3)],
        [(r, s, 3)]
        + [(at(zz, 0), at(zz, 1), 3) for zz in (1, 3)]
        + [(at(zz, 1), at(zz, 0), 0) for zz in (1, 3)],
    ]
    root_v, root_w = [1, 3, 2, None], [0, 2, 1, 3]
    dn, n3, ys = {}, {}, {}
    order, table = [], []

    def move(value, plan, kind, t):
        order.append((kind, t))
        line = [-1] * 8
        for _, target, block in plan:
            line[target] = block
        table.append(line)
        return lax.ppermute(value, "col", [(a, b) for a, b, _ in plan])

    def have(last):
        made = {"dn": dn, "n3": n3, "y": ys}
        keys = [i for i, (_, t) in enumerate(order) if t <= last]
        lines = jnp.asarray([table[i] for i in keys] + [[0] + [-1] * 7], jnp.int32)
        bufs = [made[order[i][0]][order[i][1]] for i in keys] + [panel]
        return lines.reshape(-1), one(col), 8, bufs

    def quarter(i):
        rows = source[i * n : (i + 1) * n]
        return jnp.concatenate([rows, weights if i == 2 else jnp.zeros_like(weights)], 0)

    source = panel
    tri = panel[:n, :half]
    everyone = ("row", "col")
    for t in range(4):
        if t == 0:
            weights = jnp.zeros((8, nb), jnp.float32)
            v = quarter(1)
            (source,) = fence(panel)
            w = quarter(0)
        else:
            v = dn[t - 1] if t == 3 else jnp.where(is_side, ys[t - 1], dn[t - 1])
            if root_v[t] is not None:
                v = jnp.where(is_root, quarter(root_v[t]), v)
            from_dn, source, weights = fence(dn[t - 1], source, weights)
            w = jnp.where(z == 3, n3[t - 1], from_dn) if t > 1 else from_dn
            w = jnp.where(is_root, quarter(root_w[t]), w)
        dn[t] = move(v, plan_dn[t], "dn", t)
        if plan_n3[t]:
            n3[t] = move(v, plan_n3[t], "n3", t)
        ys[t] = move(w, plan_y[t], "y", t)
        extra = []
        if t == 0:
            weights = panel_sums(panel, row, nb)
            for bit in (1, 2):
                weights += send(weights, [(i, i ^ bit) for i in range(4)])
            picked, listed = gather_rows(row, pivots, matrix)
            base = send(picked, core)
            extra = [source]
        if t == 1:
            first = jnp.where(high, half, 0)
            cut = lambda x: lax.dynamic_slice_in_dim(x, first, half, 0)
            piece = jnp.where(cut(from_core[:, None]), cut(base), cut(picked))
            near = send(piece, across_x)
            tri1 = lax.ppermute(tri, everyone, [(r, at(1, 0))])
            tri3 = lax.ppermute(tri, everyone, [(r, at(3, 0))])
        if t == 2:
            extra = [tri1, tri3, which]
        groups = [d for d in (dn, n3, ys) if t in d]
        if t < 3:
            fenced = list(fence(*[d[t] for d in groups], *extra))
            for d in groups:
                d[t] = fenced.pop(0)
            if t == 0:
                (source,) = fenced
            elif t == 2:
                tri1, tri3, which = fenced
    lines, where, stride, bufs = have(2)
    lines = jnp.concatenate([lines[:-8], jnp.asarray([-1] * 16 + [0] + [-1] * 7, jnp.int32)])
    lines = lines.at[len(bufs) * 8 - 8 + at(1, 0)].set(0).at[len(bufs) * 8 + at(3, 0)].set(0)
    below = nb // BLOCK * (nb // BLOCK - 1) // 2 * BLOCK
    packed = pl.pallas_call(
        functools.partial(pack_kernel, n, stride),
        out_shape=jax.ShapeDtypeStruct((nb + below, BLOCK), jnp.float32),
        in_specs=[smem()] * 2 + [anyspace()] * (len(bufs) + 2),
        out_specs=vmem(),
        scratch_shapes=[pltpu.SemaphoreType.DMA((nb // BLOCK * (nb // BLOCK + 1) // 2,))],
        cost_estimate=pl.CostEstimate(flops=0, bytes_accessed=8 * n * nb, transcendentals=0),
    )(lines, where, *bufs[:-1], tri1, tri3, panel)
    far = send(packed, [(0, 2)])
    other = send(near, core)
    close = send(jnp.where(row == 2, far, packed), [(0, 1), (2, 3)])
    inverse = pl.pallas_call(
        invert_diag_kernel,
        out_shape=jax.ShapeDtypeStruct((nb, BLOCK), jnp.float32),
        in_specs=[smem()] + [anyspace()] * 3,
        out_specs=vmem(),
        scratch_shapes=[pltpu.VMEM((nb, BLOCK), jnp.float32), pltpu.SemaphoreType.DMA],
        cost_estimate=pl.CostEstimate(flops=10**9, bytes_accessed=nb * nb * 4, transcendentals=0),
    )(one(row), packed, far, close)
    lines, where, stride, bufs = have(3)
    cols = matrix.shape[1]
    strip = 256 if cols % 256 == 0 else cols
    count = len(bufs) - 1
    bf, f32 = jnp.bfloat16, jnp.float32
    return pl.pallas_call(
        functools.partial(
            finish_kernel, 1.0 / float((local_rows * 4) ** 0.5), strip, n, 2, stride, count
        ),
        out_shape=(
            jax.ShapeDtypeStruct(matrix.shape, f32),
            jax.ShapeDtypeStruct((cols,), f32),
        ),
        in_specs=[smem()] * 5 + [vmem()] * 3 + [anyspace()] * (count + 10),
        out_specs=(anyspace(), vmem()),
        scratch_shapes=[
            pltpu.VMEM((nb, cols), f32),
            pltpu.VMEM((nb, cols), f32),
            pltpu.VMEM((nb, cols), f32),
            pltpu.VMEM(panel.shape, f32),
            pltpu.VMEM((local_rows, 3 * nb), bf),
            pltpu.VMEM((8, nb), f32),
            pltpu.VMEM(matrix.shape, f32),
            pltpu.VMEM((3 * nb, cols), bf),
            pltpu.VMEM((nb, 3 * nb), bf),
            pltpu.VMEM((nb, 3 * BLOCK), bf),
            pltpu.VMEM(matrix.shape, f32),
            pltpu.VMEM((below, BLOCK), f32),
            pltpu.VMEM((8, cols), f32),
            pltpu.SemaphoreType.DMA((4 * (nb // BLOCK) + 2,)),
            pltpu.SemaphoreType.DMA((count + 1,)),
            pltpu.SemaphoreType.DMA((count + 1,)),
            pltpu.SemaphoreType.DMA((cols // strip * (local_rows // nb),)),
        ],
    )(
        one(row), pivots, listed, lines, where, which, inverse, checks,
        *bufs[:-1], panel, weights, picked, base, near, other, matrix, packed, far, close,
    )


def local(matrix, panel_lower, pivots, checks):
    local_rows, local_cols = matrix.shape
    nb = pivots.shape[0]
    n_row, n_col = lax.axis_size("row"), lax.axis_size("col")
    row = lax.axis_index("row")
    special = n_row == 4 and n_col == 8 and nb == local_rows // 2
    if special:
        return step_4x8(panel_lower[0], matrix, pivots, checks)
    pieces, picked, swapped, diag = exchange(panel_lower[0], matrix, pivots)
    inverse = pl.pallas_call(
        invert_kernel,
        out_shape=jax.ShapeDtypeStruct((nb, BLOCK), jnp.float32),
        in_specs=[vmem()],
        out_specs=vmem(),
        cost_estimate=pl.CostEstimate(flops=10**9, bytes_accessed=nb * nb * 4, transcendentals=0),
    )(diag)
    lower, weights = split_panel(*pieces)
    strip = 256 if local_cols % 256 == 0 else local_cols
    scale = 1.0 / float((local_rows * n_row) ** 0.5)
    bf = jnp.bfloat16
    updated, new_checks = pl.pallas_call(
        functools.partial(final_kernel, scale, strip),
        out_shape=(
            jax.ShapeDtypeStruct(matrix.shape, jnp.float32),
            jax.ShapeDtypeStruct((1, local_cols), jnp.float32),
        ),
        in_specs=[smem()] + [vmem()] * 3 + [anyspace(), vmem(), anyspace(), vmem()],
        out_specs=(anyspace(), vmem()),
        scratch_shapes=[
            pltpu.VMEM((3 * nb, local_cols), bf),
            pltpu.VMEM((nb, 3 * nb), bf),
            pltpu.VMEM((nb, 3 * BLOCK), bf),
            pltpu.VMEM(matrix.shape, jnp.float32),
            pltpu.VMEM(lower.shape, bf),
            pltpu.VMEM(matrix.shape, jnp.float32),
            pltpu.SemaphoreType.DMA((2,)),
            pltpu.SemaphoreType.DMA((local_cols // strip * (local_rows // nb),)),
        ],
    )(
        jnp.where(row == 0, 1, 0).astype(jnp.int32)[None],
        picked,
        diag,
        inverse,
        lower,
        weights,
        swapped,
        checks[None, :],
    )
    return updated, new_checks[0]


def solution(mesh):
    return jax.shard_map(
        local,
        mesh=mesh,
        in_specs=(P("row", "col"), P("col", "row", None), P(), P("col")),
        out_specs=(P("row", "col"), P("col")),
        check_vma=False,
    )
```

```python
import functools

import jax
import jax.numpy as jnp
from jax import lax
from jax.experimental import pallas as pl
from jax.experimental.pallas import tpu as pltpu
from jax.sharding import PartitionSpec as P


BLOCK = 128
CHUNKS = 4
LAG = 1


def split(x):
    hi = x.astype(jnp.bfloat16)
    return hi, (x - hi.astype(jnp.float32)).astype(jnp.bfloat16)


def bdot(a, b):
    return jnp.dot(a, b, preferred_element_type=jnp.float32)


def vmem():
    return pl.BlockSpec(memory_space=pltpu.VMEM)


def smem():
    return pl.BlockSpec(memory_space=pltpu.SMEM)


def gather_kernel(rank, pivots, m, o, listed):
    nb, height = o.shape[0], m.shape[0]
    start = rank[0] * height

    def group(g, found):
        for i in range(8):
            k = g * 8 + i
            d = pivots[k] - start
            ours = (d >= 0) & (d < height)
            o[pl.ds(k, 1), :] = m[pl.ds(jnp.where(ours, d, k), 1), :]
            listed[found] = k
            found += (ours & (pivots[k] >= nb)).astype(jnp.int32)
        return found

    listed[nb] = lax.fori_loop(0, nb // 8, group, 0)


def move_rows(rank, pivots, listed, nb, u, o):
    start = rank[0] * o.shape[0]

    def one(i, c):
        k = listed[i]
        o[pl.ds(pivots[k] - start, 1), :] = u[pl.ds(k, 1), :]
        return c

    lax.fori_loop(0, listed[nb], one, 0)


def scatter_kernel(rank, pivots, listed, m, u, o):
    o[...] = m[...]
    move_rows(rank, pivots, listed, u.shape[0], u, o)


def invert_blocks(diag):
    n = BLOCK
    row = lax.broadcasted_iota(jnp.int32, (n, n), 0)
    col = lax.broadcasted_iota(jnp.int32, (n, n), 1)
    eye = jnp.where(row == col, 1.0, 0.0)
    inv = None
    s = 1
    while s < n:
        mask = (row // (2 * s) == col // (2 * s)) & ((row // s) % 2 == 1) & ((col // s) % 2 == 0)
        low = [jnp.where(mask, d, 0.0) for d in diag]
        if inv is None:
            inv = [eye - c for c in low]
        else:
            right = [bdot(wide(c), tall(d)) for c, d in zip(low, inv)]
            inv = [d - bdot(wide(d), tall(t)) for d, t in zip(inv, right)]
        s *= 2
    return inv


def invert_kernel(u, o):
    n = BLOCK
    count = u.shape[0] // n
    inv = invert_blocks([u[b * n : (b + 1) * n, b * n : (b + 1) * n] for b in range(count)])
    for b in range(count):
        o[b * n : (b + 1) * n, :] = inv[b]


def blocks_below(b):
    return b * (b - 1) // 2


def pack_kernel(rows, stride, blk, at, *refs):
    *bufs, panel, o, sems = refs
    n = BLOCK
    per = rows // n

    def moves(src, base, which):
        for i in range(per):
            b = which * per + i
            for k in range(b + 1):
                part = src.at[pl.ds(base + i * n, n), pl.ds(k * n, n)]
                to = o.at[pl.ds((b if k == b else 2 * per + blocks_below(b) + k) * n, n), :]
                yield pltpu.make_async_copy(part, to, sems.at[blocks_below(b + 1) + k])

    def each(do):
        for i, buf in enumerate(bufs):
            block = blk[i * stride + at[0]]
            for which in range(2):
                if which and buf.shape[1] < 2 * rows:
                    continue

                @pl.when(block == which)
                def _(buf=buf, which=which):
                    for copy in moves(buf, 0, which):
                        do(copy)

        @pl.when(blk[len(bufs) * stride + at[0]] == 0)
        def _():
            for which in range(2):
                for copy in moves(panel, which * rows, which):
                    do(copy)

    each(lambda copy: copy.start())
    each(lambda copy: copy.wait())


def take_by_rank(rank, first, own, far, near, to, sem, do):
    rows = pl.ds(first, to.shape[0])

    @pl.when(rank[0] == 0)
    def _():
        do(pltpu.make_async_copy(own.at[rows, :], to, sem))

    @pl.when(rank[0] == 2)
    def _():
        do(pltpu.make_async_copy(far.at[rows, :], to, sem))

    @pl.when(rank[0] % 2 == 1)
    def _():
        do(pltpu.make_async_copy(near.at[rows, :], to, sem))


def invert_diag_kernel(rank, own, far, near, o, u, sem):
    take_by_rank(rank, 0, own, far, near, u, sem, lambda copy: copy.start())
    take_by_rank(rank, 0, own, far, near, u, sem, lambda copy: copy.wait())
    n = BLOCK
    count = u.shape[0] // n
    inv = invert_blocks([u[b * n : (b + 1) * n, :] for b in range(count)])
    for b in range(count):
        o[b * n : (b + 1) * n, :] = inv[b]


def fetch_kernel(rows, want, stride, blk, at, *refs):
    *bufs, panel, o, sem = refs
    for i, buf in enumerate(bufs):

        @pl.when(blk[i * stride + at[0]] == want)
        def _(buf=buf):
            copy = pltpu.make_async_copy(buf.at[pl.ds(0, rows), :], o, sem)
            copy.start()
            copy.wait()

    @pl.when(blk[len(bufs) * stride + at[0]] == 0)
    def _():
        copy = pltpu.make_async_copy(panel.at[pl.ds(want * rows, rows), :], o, sem)
        copy.start()
        copy.wait()


def split_kernel(rows, carrier, stride, blk, at, *refs):
    *bufs, panel, weights, o, sums, stage, sems, more = refs
    total = panel.shape[0]

    def copies(do):
        for i, buf in enumerate(bufs):
            block = blk[i * stride + at[0]]

            @pl.when(block >= 0)
            def _(i=i, buf=buf, block=block):
                place = pl.ds(pl.multiple_of(block * rows, rows), rows)
                do(pltpu.make_async_copy(buf.at[pl.ds(0, rows), :], stage.at[place, :], sems.at[i]))

            if carrier is not None:

                @pl.when(block == carrier)
                def _(i=i, buf=buf):
                    do(pltpu.make_async_copy(buf.at[pl.ds(rows, 8), :], sums, more.at[i]))

        @pl.when(blk[len(bufs) * stride + at[0]] == 0)
        def _():
            do(pltpu.make_async_copy(panel, stage, sems.at[len(bufs)]))
            if carrier is not None:
                do(pltpu.make_async_copy(weights, sums, more.at[len(bufs)]))

        if carrier is None:
            do(pltpu.make_async_copy(weights, sums, more.at[len(bufs)]))

    copies(lambda copy: copy.start())
    copies(lambda copy: copy.wait())
    n = BLOCK
    for r in range(0, total, n):
        for k in range(panel.shape[1] // n):
            o[r : r + n, 3 * n * k : 3 * n * (k + 1)] = wide(stage[r : r + n, k * n : (k + 1) * n])


def wide(x):
    hi, lo = split(x)
    return jnp.concatenate([hi, hi, lo], axis=1)


def tall(x):
    hi, lo = split(x)
    return jnp.concatenate([hi, lo, hi], axis=0)


def final_kernel(scale, strip, flag, p, u, inv, ll_in, w, sw_in, ck, o, nc, s3, uu, ii, ob, ll, sw, got, sent):
    arrivals = [pltpu.make_async_copy(ll_in, ll, got.at[0]), pltpu.make_async_copy(sw_in, sw, got.at[1])]
    for copy in arrivals:
        copy.start()
    nb, cols = p.shape
    n = BLOCK
    count = nb // n
    for b in range(count):
        rows = slice(b * n, (b + 1) * n)
        ii[rows, :] = wide(inv[rows, :])
        for k in range(b):
            uu[rows, 3 * n * k : 3 * n * (k + 1)] = wide(u[rows, k * n : (k + 1) * n])
    for b in range(count):
        rows = slice(b * n, (b + 1) * n)
        for c in range(0, cols, strip):
            at = slice(c, c + strip)
            x = p[rows, at]
            if b:
                x = x - bdot(uu[rows, : 3 * n * b], s3[: 3 * n * b, at])
            solved = bdot(ii[rows, :], tall(x))
            s3[3 * n * b : 3 * n * (b + 1), at] = tall(solved)
            ob[rows, at] = solved
    for copy in arrivals:
        copy.wait()
    wrows = jnp.concatenate([wide(w[:, k * n : (k + 1) * n]) for k in range(count)], axis=1)
    is_top = flag[0] == 1
    leaving = []
    for c in range(0, cols, strip):
        at = slice(c, c + strip)
        sums = jnp.sum(p[:, at] - ob[:nb, at], 0, keepdims=True) + bdot(wrows, s3[:, at])[0:1, :]
        nc[:, at] = ck[:, at] - sums * scale
        for r in range(0, sw.shape[0], nb):
            rows = slice(r, r + nb)
            value = sw[rows, at] - bdot(ll[rows, :], s3[:, at])
            if r == 0:
                value = jnp.where(is_top, ob[rows, at], value)
            ob[rows, at] = value
            copy = pltpu.make_async_copy(ob.at[rows, at], o.at[rows, at], sent.at[len(leaving)])
            copy.start()
            leaving.append(copy)
    for copy in leaving:
        copy.wait()


def finish_kernel(scale, strip, rows, carrier, stride, count, rank, pivots, listed, blk, at, which, inv, ck, *refs):
    bufs, (panel, weights, x, base, near, far, m, u0, u2, u1) = refs[:count], refs[count : count + 10]
    o, nc, picked, core, full, stage, ll, w, sw, s3, uu, ii, ob, u, sums, sems, lsem, wsem, sent = refs[count + 10 :]
    nb, half = full.shape[0], near.shape[0]
    n, cols = BLOCK, picked.shape[1]
    blocks = nb // n
    mine = pl.multiple_of((rank[0] % 2) * half, half)
    theirs = pl.multiple_of(half - mine, half)
    loads = []
    for b in range(blocks):
        rs = pl.ds(b * n, n)
        group = [(x.at[rs, :], picked.at[rs, :]), (base.at[rs, :], core.at[rs, :])]
        if b * n < half:
            group.append((near.at[rs, :], full.at[pl.ds(mine + b * n, n), :]))
            group.append((far.at[rs, :], full.at[pl.ds(theirs + b * n, n), :]))
        loads.append([pltpu.make_async_copy(src, to, sems.at[4 * b + i]) for i, (src, to) in enumerate(group)])
    whole = pltpu.make_async_copy(m, sw, sems.at[4 * blocks])
    last = sems.at[4 * blocks + 1]

    def pieces(do):
        for i, buf in enumerate(bufs):
            block = blk[i * stride + at[0]]

            @pl.when(block >= 0)
            def _(i=i, buf=buf, block=block):
                place = pl.ds(pl.multiple_of(block * rows, rows), rows)
                do(pltpu.make_async_copy(buf.at[pl.ds(0, rows), :], stage.at[place, :], lsem.at[i]))

            @pl.when(block == carrier)
            def _(i=i, buf=buf):
                do(pltpu.make_async_copy(buf.at[pl.ds(rows, 8), :], w, wsem.at[i]))

        @pl.when(blk[count * stride + at[0]] == 0)
        def _():
            do(pltpu.make_async_copy(panel, stage, lsem.at[count]))
            do(pltpu.make_async_copy(weights, w, wsem.at[count]))

    take_by_rank(rank, nb, u0, u2, u1, u, last, lambda copy: copy.start())
    for group in loads:
        for copy in group:
            copy.start()
    pieces(lambda copy: copy.start())
    whole.start()
    for b in range(blocks):
        ii[b * n : (b + 1) * n, :] = wide(inv[b * n : (b + 1) * n, :])
    take_by_rank(rank, nb, u0, u2, u1, u, last, lambda copy: copy.wait())
    for b in range(blocks):
        for k in range(b):
            r = (blocks_below(b) + k) * n
            uu[b * n : (b + 1) * n, 3 * n * k : 3 * n * (k + 1)] = wide(u[r : r + n, :])
    on_diagonal = lax.broadcasted_iota(jnp.int32, (n, n), 0) == lax.broadcasted_iota(jnp.int32, (n, n), 1)
    for b in range(blocks):
        for copy in loads[b]:
            copy.wait()
        r = slice(b * n, (b + 1) * n)
        lanes = jnp.broadcast_to(which[b : b + 1, :], (n, n))
        pick = jnp.max(jnp.where(on_diagonal, lanes, 0.0), 1, keepdims=True)
        for c in range(0, cols, strip):
            cs = slice(c, c + strip)
            p = jnp.where(pick == 2, full[r, cs], jnp.where(pick == 1, core[r, cs], picked[r, cs]))
            gained = jnp.sum(p, 0, keepdims=True)
            if b:
                p = p - bdot(uu[r, : 3 * n * b], s3[: 3 * n * b, cs])
            solved = bdot(ii[r, :], tall(p))
            s3[3 * n * b : 3 * n * (b + 1), cs] = tall(solved)
            ob[r, cs] = solved
            gained -= jnp.sum(solved, 0, keepdims=True)
            sums[0:1, cs] = gained if b == 0 else sums[0:1, cs] + gained
    whole.wait()

    @pl.when(rank[0] == 0)
    def _():
        move_rows(rank, pivots, listed, nb, sw, sw)

    @pl.when(rank[0] == 1)
    def _():
        move_rows(rank, pivots, listed, nb, core, sw)

    @pl.when(rank[0] >= 2)
    def _():
        move_rows(rank, pivots, listed, nb, full, sw)

    pieces(lambda copy: copy.wait())
    for r in range(0, sw.shape[0], n):
        for k in range(blocks):
            ll[r : r + n, 3 * n * k : 3 * n * (k + 1)] = wide(stage[r : r + n, k * n : (k + 1) * n])
    wrows = jnp.concatenate([wide(w[:, k * n : (k + 1) * n]) for k in range(blocks)], axis=1)
    is_top = rank[0] == 0
    leaving = []
    for c in range(0, cols, strip):
        cs = slice(c, c + strip)
        change = sums[0:1, cs] + bdot(wrows, s3[:, cs])[0:1, :]
        nc[cs] = ck[cs] - (change * scale).reshape(strip)
        for r in range(0, sw.shape[0], nb):
            rs = slice(r, r + nb)
            value = sw[rs, cs] - bdot(ll[rs, :], s3[:, cs])
            if r == 0:
                value = jnp.where(is_top, ob[rs, cs], value)
            ob[rs, cs] = value
            copy = pltpu.make_async_copy(ob.at[rs, cs], o.at[rs, cs], sent.at[len(leaving)])
            copy.start()
            leaving.append(copy)
    for copy in leaving:
        copy.wait()


def stream(panel, n_col, chunks, lag):
    depth = n_col // 2
    col = lax.axis_index("col")
    is_root, is_side = col == 0, col == 1
    n = panel.shape[0] // (2 * chunks)
    a = [panel[2 * j * n : (2 * j + 1) * n] for j in range(chunks)]
    b = [panel[(2 * j + 1) * n : (2 * j + 2) * n] for j in range(chunks)]
    z, y = col // 2, col % 2
    along, across = {}, {}
    blocks = {}
    for t in range(max(chunks + lag * depth, 2 * chunks)):
        z_pairs, y_pairs = [], []
        for zz in range(depth):
            for yy in range(2):
                j = t - lag * zz - lag * yy
                if 0 <= j < chunks:
                    if zz < depth - 1:
                        z_pairs.append((2 * zz + yy, 2 * zz + 2 + yy))
                    if zz > 0:
                        y_pairs.append((2 * zz + yy, 2 * zz + 1 - yy))
        if t < 2 * chunks:
            y_pairs.append((0, 1))
        before_z, before_y = along.get(t - lag), across.get(t - lag)
        if t < chunks:
            z_in = b[t] if before_z is None else jnp.where(is_root, b[t], before_z)
        else:
            z_in = before_z
        if z_in is not None and before_y is not None:
            z_in = jnp.where(is_side, before_y, z_in)
        head = a[t] if t < chunks else (b[t - chunks] if t < 2 * chunks else None)
        if head is None:
            y_in = z_in
        elif z_in is None:
            y_in = head
        else:
            y_in = jnp.where(is_root, head, z_in)
        if y_pairs:
            across[t] = lax.ppermute(y_in, "col", y_pairs)
            j = t - lag * z - lag * (1 - y)
            ok = (z > 0) & (j >= 0) & (j < chunks)
            value = jnp.where(ok, 2 * j + y, -1)
            if t < 2 * chunks:
                first = 2 * t if t < chunks else 2 * (t - chunks) + 1
                value = jnp.where(is_side, first, value)
            blocks["y", t] = value
        if z_pairs:
            along[t] = lax.ppermute(z_in, "col", z_pairs)
            j = t - lag * (z - 1) - lag * y
            ok = (z > 0) & (j >= 0) & (j < chunks)
            blocks["z", t] = jnp.where(ok, 2 * j + 1 - y, -1)
    return n, along, across, blocks, is_root


def anyspace():
    return pl.BlockSpec(memory_space=pl.ANY)


def fetch(found, rows, want):
    blk, at, stride, bufs = found
    return pl.pallas_call(
        functools.partial(fetch_kernel, rows, want, stride),
        out_shape=jax.ShapeDtypeStruct((rows, bufs[0].shape[1]), jnp.float32),
        in_specs=[smem()] * 2 + [anyspace()] * len(bufs),
        out_specs=vmem(),
        scratch_shapes=[pltpu.SemaphoreType.DMA],
        cost_estimate=pl.CostEstimate(flops=0, bytes_accessed=8 * bufs[0].size, transcendentals=0),
    )(blk, at, *bufs)


def split_panel(found, rows, carrier, weights):
    blk, at, stride, bufs = found
    panel = bufs[-1]
    return pl.pallas_call(
        functools.partial(split_kernel, rows, carrier, stride),
        out_shape=(
            jax.ShapeDtypeStruct((panel.shape[0], 3 * panel.shape[1]), jnp.bfloat16),
            jax.ShapeDtypeStruct(weights.shape, jnp.float32),
        ),
        in_specs=[smem()] * 2 + [anyspace()] * (len(bufs) + 1),
        out_specs=(vmem(), vmem()),
        scratch_shapes=[
            pltpu.VMEM(panel.shape, jnp.float32),
            pltpu.SemaphoreType.DMA((len(bufs),)),
            pltpu.SemaphoreType.DMA((len(bufs),)),
        ],
        cost_estimate=pl.CostEstimate(flops=0, bytes_accessed=10 * panel.size, transcendentals=0),
    )(blk, at, *bufs, weights)


def halves(own, other, high):
    return jnp.concatenate(
        [jnp.where(high, other, own), jnp.where(high, own, other)], axis=0
    )


def one(value):
    return value.astype(jnp.int32)[None]


def scatter_rows(row, pivots, listed, matrix, upper):
    return pl.pallas_call(
        scatter_kernel,
        out_shape=jax.ShapeDtypeStruct(matrix.shape, jnp.float32),
        in_specs=[smem(), smem(), smem(), vmem(), vmem()],
        out_specs=vmem(),
        cost_estimate=pl.CostEstimate(flops=0, bytes_accessed=8 * matrix.size, transcendentals=0),
    )(one(row), pivots, listed, matrix, upper)


def gather_rows(row, pivots, matrix):
    nb = pivots.shape[0]
    return pl.pallas_call(
        gather_kernel,
        out_shape=(
            jax.ShapeDtypeStruct((nb, matrix.shape[1]), jnp.float32),
            jax.ShapeDtypeStruct((nb + 8,), jnp.int32),
        ),
        in_specs=[smem(), smem(), vmem()],
        out_specs=(vmem(), smem()),
        cost_estimate=pl.CostEstimate(flops=0, bytes_accessed=8 * matrix.size, transcendentals=0),
    )(one(row), pivots, matrix)


def panel_sums(panel, row, nb):
    local_rows = panel.shape[0]
    global_rows = row * local_rows + jnp.arange(local_rows, dtype=jnp.int32)
    sums = jnp.sum(jnp.where((global_rows >= nb)[:, None], panel, 0.0), 0, keepdims=True)
    return jnp.broadcast_to(sums, (8, nb))


def exchange(panel, matrix, pivots):
    nb = pivots.shape[0]
    local_rows = matrix.shape[0]
    n_row, n_col = lax.axis_size("row"), lax.axis_size("col")
    row, col = lax.axis_index("row"), lax.axis_index("col")
    high = (row % 2) == 1
    owner = pivots // local_rows
    rows, along, across, blocks, is_root = stream(panel, n_col, CHUNKS, LAG)
    weights = panel_sums(panel, row, nb)
    bit = 1
    while bit < n_row:
        weights += lax.ppermute(weights, "row", [(i, i ^ bit) for i in range(n_row)])
        bit *= 2
    bit = 1
    while bit < n_col:
        moved = lax.ppermute(weights, "col", [(i, i + bit) for i in range(bit)])
        weights = jnp.where((col >= bit) & (col < 2 * bit), moved, weights)
        bit *= 2
    picked, listed = gather_rows(row, pivots, matrix)
    upper = matrix[:nb]
    half = nb // 2
    swap_all = [(i, i ^ 1) for i in range(n_row)]
    bit, level = 1, 0
    while bit < n_row:
        pairs = [(i, i ^ bit) for i in range(n_row)]
        if bit == 1:
            other = lax.ppermute(picked, "row", pairs)
        else:
            piece = lax.dynamic_slice_in_dim(picked, jnp.where(high, half, 0), half, 0)
            piece = lax.ppermute(piece, "row", pairs)
            other = halves(piece, lax.ppermute(piece, "row", swap_all), high)
        group = row >> level
        upper = jnp.where(group == 1, other, upper)
        theirs = (owner >> level) == (group ^ 1)
        outside = (owner >> level) != group
        picked = jnp.where((theirs | (outside & (group == 1)))[:, None], other, picked)
        bit, level = 2 * bit, level + 1
    blk = jnp.stack(list(blocks.values()) + [jnp.where(is_root, 0, -1)]).astype(jnp.int32)
    bufs = [(across if kind == "y" else along)[t] for kind, t in blocks] + [panel]
    found = blk, jnp.zeros((1,), jnp.int32), 1, bufs
    diag = jnp.concatenate([fetch(found, rows, b) for b in range(nb // rows)], 0)
    moved = lax.ppermute(diag, "row", [(0, 1)])
    diag = jnp.where(row == 1, moved, diag)
    bit = 2
    while bit < n_row:
        piece = lax.dynamic_slice_in_dim(diag, jnp.where(high, half, 0), half, 0)
        piece = lax.ppermute(piece, "row", [(i, i + bit) for i in range(bit)])
        other = lax.ppermute(piece, "row", [(i, i ^ 1) for i in range(bit, 2 * bit)])
        diag = jnp.where((row >= bit) & (row < 2 * bit), halves(piece, other, high), diag)
        bit *= 2
    swapped = scatter_rows(row, pivots, listed, matrix, upper)
    return (found, rows, None, weights), picked, swapped, diag


def fence(*values):
    return lax.optimization_barrier(values)


def step_4x8(panel, matrix, pivots, checks):
    nb = pivots.shape[0]
    local_rows = matrix.shape[0]
    row, col = lax.axis_index("row"), lax.axis_index("col")
    z = col // 2
    high = (row % 2) == 1
    is_root, is_side = col == 0, col == 1
    n = local_rows // 4
    at = lambda zz, yy: 2 * zz + yy
    owner = pivots // local_rows
    half = nb // 2
    in_pair = (owner >> 1) == (row >> 1)
    from_core = (owner == (row ^ 1)) | (~in_pair & (row == 1))
    which = jnp.where(in_pair, jnp.where(owner == row, 0.0, 1.0), 2.0).reshape(nb // BLOCK, BLOCK)
    core = [(i, i ^ 1) for i in range(4)]
    across_x = [(i, i ^ 2) for i in range(4)]
    send = lambda x, pairs: lax.ppermute(x, "row", pairs)
    r, s = at(0, 0), at(0, 1)
    plan_dn = [
        [(r, at(2, 0), 1)],
        [(r, at(2, 0), 3), (s, at(2, 1), 0), (at(2, 0), at(1, 0), 1)],
        [(r, at(2, 0), 2), (s, at(2, 1), 2), (at(2, 0), at(1, 0), 3), (at(2, 1), at(1, 1), 0)],
        [(at(2, 0), at(1, 0), 2), (at(2, 1), at(1, 1), 2)],
    ]
    plan_n3 = [
        [],
        [(at(2, 0), at(3, 0), 1)],
        [(at(2, 0), at(3, 0), 3), (at(2, 1), at(3, 1), 0)],
        [(at(2, 0), at(3, 0), 2), (at(2, 1), at(3, 1), 2)],
    ]
    plan_y = [
        [(r, s, 0)],
        [(r, s, 2), (at(2, 0), at(2, 1), 1)],
        [(r, s, 1), (at(2, 0), at(2, 1), 3), (at(2, 1), at(2, 0), 0)]
        + [(at(zz, 0), at(zz, 1), 1) for zz in (1, 3)],
        [(r, s, 3)]
        + [(at(zz, 0), at(zz, 1), 3) for zz in (1, 3)]
        + [(at(zz, 1), at(zz, 0), 0) for zz in (1, 3)],
    ]
    root_v, root_w = [1, 3, 2, None], [0, 2, 1, 3]
    dn, n3, ys = {}, {}, {}
    order, table = [], []

    def move(value, plan, kind, t):
        order.append((kind, t))
        line = [-1] * 8
        for _, target, block in plan:
            line[target] = block
        table.append(line)
        return lax.ppermute(value, "col", [(a, b) for a, b, _ in plan])

    def have(last):
        made = {"dn": dn, "n3": n3, "y": ys}
        keys = [i for i, (_, t) in enumerate(order) if t <= last]
        lines = jnp.asarray([table[i] for i in keys] + [[0] + [-1] * 7], jnp.int32)
        bufs = [made[order[i][0]][order[i][1]] for i in keys] + [panel]
        return lines.reshape(-1), one(col), 8, bufs

    def quarter(i):
        rows = source[i * n : (i + 1) * n]
        return jnp.concatenate([rows, weights if i == 2 else jnp.zeros_like(weights)], 0)

    source, held = panel, {}
    tri = panel[:n, :half]
    everyone = ("row", "col")
    for t in range(4):
        if t == 0:
            weights = jnp.zeros((8, nb), jnp.float32)
            v = quarter(1)
            (source,) = fence(panel)
            w = quarter(0)
        else:
            v = dn[t - 1] if t == 3 else jnp.where(is_side, ys[t - 1], dn[t - 1])
            kept = held.get(root_v[t])
            if root_v[t] is not None:
                v = jnp.where(is_root, quarter(root_v[t]) if kept is None else kept, v)
            from_dn, source, weights = fence(dn[t - 1], source, weights)
            w = jnp.where(z == 3, n3[t - 1], from_dn) if t > 1 else from_dn
            kept = held.get(root_w[t])
            w = jnp.where(is_root, quarter(root_w[t]) if kept is None else kept, w)
        held[root_v[t]], held[root_w[t]] = v, w
        dn[t] = move(v, plan_dn[t], "dn", t)
        if plan_n3[t]:
            n3[t] = move(v, plan_n3[t], "n3", t)
        ys[t] = move(w, plan_y[t], "y", t)
        extra = []
        if t == 0:
            weights = panel_sums(panel, row, nb)
            for bit in (1, 2):
                weights += send(weights, [(i, i ^ bit) for i in range(4)])
            picked, listed = gather_rows(row, pivots, matrix)
            base = send(picked, core)
            extra = [source]
        if t == 1:
            first = jnp.where(high, half, 0)
            cut = lambda x: lax.dynamic_slice_in_dim(x, first, half, 0)
            piece = jnp.where(cut(from_core[:, None]), cut(base), cut(picked))
            near = send(piece, across_x)
            tri1 = lax.ppermute(tri, everyone, [(r, at(1, 0))])
            tri3 = lax.ppermute(tri, everyone, [(r, at(3, 0))])
        if t == 2:
            extra = [tri1, tri3, which]
        groups = [d for d in (dn, n3, ys) if t in d]
        if t < 3:
            fenced = list(fence(*[d[t] for d in groups], *extra))
            for d in groups:
                d[t] = fenced.pop(0)
            if t == 0:
                (source,) = fenced
            elif t == 2:
                tri1, tri3, which = fenced
    lines, where, stride, bufs = have(2)
    lines = jnp.concatenate([lines[:-8], jnp.asarray([-1] * 16 + [0] + [-1] * 7, jnp.int32)])
    lines = lines.at[len(bufs) * 8 - 8 + at(1, 0)].set(0).at[len(bufs) * 8 + at(3, 0)].set(0)
    below = nb // BLOCK * (nb // BLOCK - 1) // 2 * BLOCK
    packed = pl.pallas_call(
        functools.partial(pack_kernel, n, stride),
        out_shape=jax.ShapeDtypeStruct((nb + below, BLOCK), jnp.float32),
        in_specs=[smem()] * 2 + [anyspace()] * (len(bufs) + 2),
        out_specs=vmem(),
        scratch_shapes=[pltpu.SemaphoreType.DMA((nb // BLOCK * (nb // BLOCK + 1) // 2,))],
        cost_estimate=pl.CostEstimate(flops=0, bytes_accessed=8 * n * nb, transcendentals=0),
    )(lines, where, *bufs[:-1], tri1, tri3, panel)
    far = send(packed, [(0, 2)])
    other = send(near, core)
    close = send(jnp.where(row == 2, far, packed), [(0, 1), (2, 3)])
    inverse = pl.pallas_call(
        invert_diag_kernel,
        out_shape=jax.ShapeDtypeStruct((nb, BLOCK), jnp.float32),
        in_specs=[smem()] + [anyspace()] * 3,
        out_specs=vmem(),
        scratch_shapes=[pltpu.VMEM((nb, BLOCK), jnp.float32), pltpu.SemaphoreType.DMA],
        cost_estimate=pl.CostEstimate(flops=10**9, bytes_accessed=nb * nb * 4, transcendentals=0),
    )(one(row), packed, far, close)
    lines, where, stride, bufs = have(3)
    cols = matrix.shape[1]
    strip = 256 if cols % 256 == 0 else cols
    count = len(bufs) - 1
    bf, f32 = jnp.bfloat16, jnp.float32
    return pl.pallas_call(
        functools.partial(
            finish_kernel, 1.0 / float((local_rows * 4) ** 0.5), strip, n, 2, stride, count
        ),
        out_shape=(
            jax.ShapeDtypeStruct(matrix.shape, f32),
            jax.ShapeDtypeStruct((cols,), f32),
        ),
        in_specs=[smem()] * 5 + [vmem()] * 3 + [anyspace()] * (count + 10),
        out_specs=(anyspace(), vmem()),
        scratch_shapes=[
            pltpu.VMEM((nb, cols), f32),
            pltpu.VMEM((nb, cols), f32),
            pltpu.VMEM((nb, cols), f32),
            pltpu.VMEM(panel.shape, f32),
            pltpu.VMEM((local_rows, 3 * nb), bf),
            pltpu.VMEM((8, nb), f32),
            pltpu.VMEM(matrix.shape, f32),
            pltpu.VMEM((3 * nb, cols), bf),
            pltpu.VMEM((nb, 3 * nb), bf),
            pltpu.VMEM((nb, 3 * BLOCK), bf),
            pltpu.VMEM(matrix.shape, f32),
            pltpu.VMEM((below, BLOCK), f32),
            pltpu.VMEM((8, cols), f32),
            pltpu.SemaphoreType.DMA((4 * (nb // BLOCK) + 2,)),
            pltpu.SemaphoreType.DMA((count + 1,)),
            pltpu.SemaphoreType.DMA((count + 1,)),
            pltpu.SemaphoreType.DMA((cols // strip * (local_rows // nb),)),
        ],
    )(
        one(row), pivots, listed, lines, where, which, inverse, checks,
        *bufs[:-1], panel, weights, picked, base, near, other, matrix, packed, far, close,
    )


def local(matrix, panel_lower, pivots, checks):
    local_rows, local_cols = matrix.shape
    nb = pivots.shape[0]
    n_row, n_col = lax.axis_size("row"), lax.axis_size("col")
    row = lax.axis_index("row")
    special = n_row == 4 and n_col == 8 and nb == local_rows // 2
    if special:
        return step_4x8(panel_lower[0], matrix, pivots, checks)
    pieces, picked, swapped, diag = exchange(panel_lower[0], matrix, pivots)
    inverse = pl.pallas_call(
        invert_kernel,
        out_shape=jax.ShapeDtypeStruct((nb, BLOCK), jnp.float32),
        in_specs=[vmem()],
        out_specs=vmem(),
        cost_estimate=pl.CostEstimate(flops=10**9, bytes_accessed=nb * nb * 4, transcendentals=0),
    )(diag)
    lower, weights = split_panel(*pieces)
    strip = 256 if local_cols % 256 == 0 else local_cols
    scale = 1.0 / float((local_rows * n_row) ** 0.5)
    bf = jnp.bfloat16
    updated, new_checks = pl.pallas_call(
        functools.partial(final_kernel, scale, strip),
        out_shape=(
            jax.ShapeDtypeStruct(matrix.shape, jnp.float32),
            jax.ShapeDtypeStruct((1, local_cols), jnp.float32),
        ),
        in_specs=[smem()] + [vmem()] * 3 + [anyspace(), vmem(), anyspace(), vmem()],
        out_specs=(anyspace(), vmem()),
        scratch_shapes=[
            pltpu.VMEM((3 * nb, local_cols), bf),
            pltpu.VMEM((nb, 3 * nb), bf),
            pltpu.VMEM((nb, 3 * BLOCK), bf),
            pltpu.VMEM(matrix.shape, jnp.float32),
            pltpu.VMEM(lower.shape, bf),
            pltpu.VMEM(matrix.shape, jnp.float32),
            pltpu.SemaphoreType.DMA((2,)),
            pltpu.SemaphoreType.DMA((local_cols // strip * (local_rows // nb),)),
        ],
    )(
        jnp.where(row == 0, 1, 0).astype(jnp.int32)[None],
        picked,
        diag,
        inverse,
        lower,
        weights,
        swapped,
        checks[None, :],
    )
    return updated, new_checks[0]


def solution(mesh):
    return jax.shard_map(
        local,
        mesh=mesh,
        in_specs=(P("row", "col"), P("col", "row", None), P(), P("col")),
        out_specs=(P("row", "col"), P("col")),
        check_vma=False,
    )
```
